32 devices in a mesh: img: 4 (over z), cap: 8 (over y, x, core).
Axes of the slice: x: 2, y: 2, z: 4, core: 2. Of those that a mesh axis runs over, the one named last changes fastest.
Arguments:
- patches: bfloat16 [128, 256, 768], P(('img', 'cap')), may hold values from -32 to 32
- words: bfloat16 [128, 64, 768], P(('img', 'cap')), may hold values from -4.5 to 4.5
- natural_sharpness_exponent: float32 [1], replicated, may hold values from 2.3 to 3.9
- candidates: int32 [4, 8, 6], replicated, may hold values from -1 to 7, as said below
- counts: int32 [4, 8], replicated, may hold values from 3 to 6, as said below
Outputs:
- patch_grad: bfloat16 [128, 256, 768], P(('img', 'cap'))
- word_grad: bfloat16 [128, 64, 768], P(('img', 'cap'))
- loss: float32 [1], replicated
- temp_grad: float32 [1], replicated
The draws below stay inside these ranges and needn't reach their ends.
Inputs may be any that keep to these rules, and one draw needn't show every extreme that they name: `candidates`: entry [a, b, 0] is b; entries 1 to counts[a, b] - 1 are distinct columns other than b; later entries are -1. `counts`: some image block has exactly 6 candidate blocks.
All inputs are finite; a program needn't handle non-finite values.
Results may differ from the reference program's by a relative error of at most 0.0085.
Values may be sent and summed in bfloat16 or wider, within the bound.
No kernel may reach another device: no remote copies, remote signals or barrier semaphores. Data moves between devices by JAX's collectives and lax.ppermute only.
A program may use at most 128 MiB of HBM per device.

```python
import jax
import jax.numpy as jnp
from jax import lax

D = 768
P_SIZE = 256
W = 64
IMG_DEV = 4
IMG_ROWS = 4
CAP_BLOCKS = 8
KMAX = 6
IMAGES = 128


def token_pair(key):
    word_key = jax.random.fold_in(key, 11)
    patch_key = jax.random.fold_in(key, 12)
    word_tokens = jax.random.truncated_normal(word_key, -4.0, 4.0, (IMAGES, W, D), jnp.float32)
    patch_tokens = jax.random.truncated_normal(patch_key, -4.0, 4.0, (IMAGES, P_SIZE, D), jnp.float32)
    return (patch_tokens, word_tokens)


def draw_patches(key, part):
    return token_pair(key)[0].astype(jnp.bfloat16)


def draw_words(key, part):
    return token_pair(key)[1].astype(jnp.bfloat16)


def candidate_lists(key):
    blocks = IMG_ROWS * CAP_BLOCKS
    first_key = jax.random.fold_in(key, 21)
    second_key = jax.random.fold_in(key, 22)
    pick_key = jax.random.fold_in(key, 23)
    order_key = jax.random.fold_in(key, 24)
    first_draw = jax.random.randint(first_key, (blocks,), 0, KMAX, dtype=jnp.int32)
    second_draw = jax.random.randint(second_key, (blocks,), 0, KMAX, dtype=jnp.int32)
    count_draw = jnp.minimum(KMAX // 2 + first_draw * second_draw // (KMAX - 1), KMAX)
    fullest = jax.random.randint(pick_key, (), 0, blocks, dtype=jnp.int32)
    block_ids = jnp.arange(blocks, dtype=jnp.int32)
    count_draw = jnp.where(block_ids == fullest, KMAX, count_draw).astype(jnp.int32)
    key_list = jax.random.split(order_key, blocks)
    orders = jax.vmap(lambda subkey: jax.random.permutation(subkey, CAP_BLOCKS - 1))(key_list).astype(jnp.int32)
    own_block = block_ids % CAP_BLOCKS
    others = (own_block[:, None] + 1 + orders[:, :KMAX - 1]) % CAP_BLOCKS
    cand_lists = jnp.concatenate([own_block[:, None], others], axis=1)
    slot_ids = jnp.arange(KMAX, dtype=jnp.int32)
    cand_lists = jnp.where(slot_ids[None, :] < count_draw[:, None], cand_lists, -1).astype(jnp.int32)
    return (cand_lists.reshape(IMG_ROWS, CAP_BLOCKS, KMAX), count_draw.reshape(IMG_ROWS, CAP_BLOCKS))


def draw_candidates(key, part):
    return candidate_lists(key)[0]


def draw_counts(key, part):
    return candidate_lists(key)[1]


def setup_inputs(seed: int = 0) -> dict:
    seeds = jax.random.split(jax.random.key(seed), 6)
    return {
        "patches": draw_patches(jax.random.fold_in(seeds[5], 71), 0),
        "words": draw_words(jax.random.fold_in(seeds[5], 71), 0),
        "natural_sharpness_exponent": jnp.clip(jax.random.uniform(seeds[2], (1,), jnp.float32, 2.3, 3.9), 2.3, 3.9),
        "candidates": draw_candidates(jax.random.fold_in(seeds[5], 71), 0),
        "counts": draw_counts(jax.random.fold_in(seeds[5], 71), 0),
    }


sharpness = 4.0
loss_scale = 65536.0
far_below = -1e+30

def similarity_table(patch_block, word_tile_block):
    product = jnp.einsum('ipd,jwd->ijwp', patch_block.astype(jnp.float32), word_tile_block.astype(jnp.float32), precision=lax.Precision.HIGHEST)
    return product * D ** (-0.5)

def couple_similarity_lines(linear_shift_map):
    lifted = sharpness * linear_shift_map
    over_words = jax.nn.logsumexp(lifted, axis=2) / sharpness
    over_patches = jax.nn.logsumexp(lifted, axis=3) / sharpness
    return 0.5 * (lax.optimization_barrier(jnp.mean(over_words, axis=2)) + lax.optimization_barrier(jnp.mean(over_patches, axis=2)))

def token_weights(linear_shift_map, couple_derivative):
    lifted = sharpness * linear_shift_map
    share_words = jax.nn.softmax(lifted, axis=2)
    share_patches = jax.nn.softmax(lifted, axis=3)
    blended = 0.5 * (share_words / P_SIZE + share_patches / W)
    return (blended * (couple_derivative[:, :, None, None] * (loss_scale * D ** (-0.5)))).astype(jnp.bfloat16)

def reference(patches, words, natural_sharpness_exponent, candidates, counts):
    trained_softness = jnp.exp(natural_sharpness_exponent[0])
    blocks = IMG_ROWS * CAP_BLOCKS
    region_piece_window = patches.reshape(blocks, IMG_DEV, P_SIZE, D)
    lexeme_piece_window = words.reshape(blocks, IMG_DEV, W, D)
    cand_flat = candidates.reshape(blocks, KMAX)
    count_flat = counts.reshape(blocks)
    slot_ids = jnp.arange(KMAX).astype(jnp.int32)
    block_range = jnp.arange(blocks).astype(jnp.int32)
    columns = jnp.arange(CAP_BLOCKS).astype(jnp.int32)

    def forward_block(group_index):
        row_id = group_index // CAP_BLOCKS

        def slot_scores_of(slot_index):
            column = jnp.maximum(cand_flat[group_index, slot_index], 0)
            correct_classes = row_id * CAP_BLOCKS + column

            def compute():
                return trained_softness * couple_similarity_lines(similarity_table(region_piece_window[group_index], lexeme_piece_window[correct_classes]))

            def nothing():
                return jnp.zeros((IMG_DEV, IMG_DEV), jnp.float32)
            return lax.cond(slot_index < count_flat[group_index], compute, nothing)
        return lax.map(slot_scores_of, slot_ids)
    slot_logits = lax.map(forward_block, block_range)
    live_slots = slot_ids[None, :] < count_flat[:, None]
    onehot = ((cand_flat[:, :, None] == columns[None, None, :]) & live_slots[:, :, None]).astype(jnp.float32)
    live_blocks = lax.optimization_barrier(jnp.max(onehot, axis=1))
    dense_logits = jnp.einsum('bkc,bkij->bicj', onehot, slot_logits, precision=lax.Precision.HIGHEST)
    logits = dense_logits.reshape(IMG_ROWS, CAP_BLOCKS, IMG_DEV, CAP_BLOCKS, IMG_DEV)
    live_five = live_blocks.reshape(IMG_ROWS, CAP_BLOCKS, 1, CAP_BLOCKS, 1) > 0
    masked = jnp.where(live_five, logits, far_below)
    row_lse = jax.nn.logsumexp(masked, axis=(3, 4))
    col_lse = jax.nn.logsumexp(masked, axis=(1, 2))
    eye_blocks = jnp.eye(CAP_BLOCKS, dtype=jnp.float32)
    eye_rows = jnp.eye(IMG_DEV, dtype=jnp.float32)
    positive = eye_blocks[None, :, None, :, None] * eye_rows[None, None, :, None, :]
    diagonal = jnp.sum(logits * positive)
    loss = 0.5 * (jnp.sum(row_lse) + jnp.sum(col_lse) - 2.0 * diagonal) / IMAGES
    couple_derivative = jnp.where(live_five, 0.5 / IMAGES * (jnp.exp(masked - row_lse[:, :, :, None, None]) + jnp.exp(masked - col_lse[:, None, None, :, :]) - 2.0 * positive), 0.0)
    temp_grad = jnp.sum(couple_derivative * logits)
    similarity_derivative = trained_softness * couple_derivative
    grad_view = similarity_derivative.reshape(blocks, IMG_DEV, CAP_BLOCKS, IMG_DEV)
    live_rows = live_blocks.reshape(IMG_ROWS, CAP_BLOCKS, CAP_BLOCKS)

    def patch_block_grad(group_index):
        patch_block = region_piece_window[group_index]
        row_id = group_index // CAP_BLOCKS

        def scan_step(running, slot_index):
            column = jnp.maximum(cand_flat[group_index, slot_index], 0)
            word_tile_block = lexeme_piece_window[row_id * CAP_BLOCKS + column]

            def compute(current):
                weights = token_weights(similarity_table(patch_block, word_tile_block), grad_view[group_index][:, column, :])
                return current + jnp.einsum('ijwp,jwd->ipd', weights.astype(jnp.float32), word_tile_block.astype(jnp.float32), precision=lax.Precision.HIGHEST)
            return (lax.cond(slot_index < count_flat[group_index], compute, lambda current: current, running), None)
        running, _ = lax.scan(scan_step, jnp.zeros((IMG_DEV, P_SIZE, D), jnp.float32), slot_ids)
        return running

    def word_block_grad(correct_classes):
        row_id = correct_classes // CAP_BLOCKS
        column = correct_classes % CAP_BLOCKS
        word_tile_block = lexeme_piece_window[correct_classes]

        def scan_step(running, source):
            anchor = row_id * CAP_BLOCKS + source

            def compute(current):
                patch_block = region_piece_window[anchor]
                weights = token_weights(similarity_table(patch_block, word_tile_block), similarity_derivative.reshape(IMG_ROWS, CAP_BLOCKS, IMG_DEV, CAP_BLOCKS, IMG_DEV)[row_id, source, :, column, :])
                return current + jnp.einsum('ijwp,ipd->jwd', weights.astype(jnp.float32), patch_block.astype(jnp.float32), precision=lax.Precision.HIGHEST)
            return (lax.cond(live_rows[row_id, source, column] > 0, compute, lambda current: current, running), None)
        running, _ = lax.scan(scan_step, jnp.zeros((IMG_DEV, W, D), jnp.float32), columns)
        return running
    patch_grad = lax.map(patch_block_grad, block_range).reshape(IMAGES, P_SIZE, D).astype(jnp.bfloat16)
    word_grad = lax.map(word_block_grad, block_range).reshape(IMAGES, W, D).astype(jnp.bfloat16)
    return (patch_grad, word_grad, loss.reshape(1), temp_grad.reshape(1))
```

```python
import functools
import math

import jax
import jax.numpy as jnp
from jax import lax
from jax.experimental import pallas as pl
from jax.experimental.pallas import tpu as pltpu
from jax.sharding import PartitionSpec as P

sharpness = 4.0
loss_scale = 65536.0
far_below = -1e30
F32 = jnp.float32
BF16 = jnp.bfloat16
LANES = 128
ROWS = 8
VMEM_LIMIT = 56 << 20

NT = (((1,), (1,)), ((), ()))
NN = (((1,), (0,)), ((), ()))
TN = (((0,), (0,)), ((), ()))


def spec(space=pltpu.VMEM):
    return pl.BlockSpec(memory_space=space)


def block_is_live(cands, counts, row, block, column, slots):
    live = jnp.int32(0)
    for s in range(slots):
        hit = (cands[row, block, s] == column) & (s < counts[row, block])
        live = live | hit.astype(jnp.int32)
    return live > 0


def forward_kernel(offset, cands, counts, patches, words, prior, weights_out, scores_out, low, high):
    row = lax.axis_index("img")
    me = lax.axis_index("cap")
    column = me ^ offset
    per, patch, width = patches.shape
    tokens = words.shape[1]
    lines = per * tokens
    scale = sharpness * width**-0.5 * math.log2(math.e)
    scores_out[...] = prior[...]

    @pl.when(block_is_live(cands, counts, row, me, column, cands.shape[2]))
    def _():
        sub = lax.broadcasted_iota(jnp.int32, (ROWS, LANES), 0)
        lane = lax.broadcasted_iota(jnp.int32, (ROWS, LANES), 1)
        spot = lane == column * per + sub

        def place(i, over_words, over_patches):
            part = jnp.sum(over_words, axis=1, keepdims=True) * (1.0 / patch)
            part = part + over_patches * (1.0 / tokens)
            part = part * (0.5 * math.log(2.0) / sharpness)
            part = jnp.concatenate([part, jnp.zeros((ROWS - per, 1), F32)], axis=0)
            line = jnp.sum(jnp.where(spot & (sub < per), part, 0.0), axis=0, keepdims=True)
            return jnp.where(sub == i, line, 0.0)

        word_rows = words[...].reshape(lines, width)
        low[...] = jnp.full(low.shape, 1.0, F32)
        high[...] = jnp.full(high.shape, 1.0, F32)
        tile = jnp.zeros((ROWS, LANES), F32)
        for i in range(per):
            raw = lax.dot_general(word_rows, patches[i], NT, preferred_element_type=F32)
            mass = jnp.exp2(raw * scale)
            mass3 = mass.reshape(per, tokens, patch)
            word_sum = jnp.sum(mass3, axis=1)
            patch_sum = jnp.sum(mass, axis=1, keepdims=True)
            low[...] = jnp.minimum(low[...], jnp.min(word_sum, axis=0, keepdims=True))
            high[...] = jnp.maximum(high[...], jnp.max(word_sum, axis=0, keepdims=True))
            low[...] = jnp.minimum(low[...], jnp.min(patch_sum, axis=0, keepdims=True))
            high[...] = jnp.maximum(high[...], jnp.max(patch_sum, axis=0, keepdims=True))
            word_part = (0.5 / patch) / word_sum
            patch_part = (0.5 / tokens) / patch_sum
            blended = mass3 * (word_part[:, None, :] + patch_part.reshape(per, tokens, 1))
            weights_out[i] = blended.reshape(lines, patch).astype(BF16)
            patch_logs = jnp.sum(jnp.log2(patch_sum).reshape(per, tokens, 1), axis=1)
            tile = tile + place(i, jnp.log2(word_sum), patch_logs)
        scores_out[...] += tile
        safe = (jnp.min(low[...]) > 2.0**-90) & (jnp.max(high[...]) < 2.0**120)

        @pl.when(jnp.logical_not(safe))
        def _():
            scores_out[...] = prior[...]

            def image(i, carry):
                raw = lax.dot_general(word_rows, patches[i], NT, preferred_element_type=F32)
                lifted = raw * scale
                lifted3 = lifted.reshape(per, tokens, patch)
                word_top = jnp.max(lifted3, axis=1)
                patch_top = jnp.max(lifted, axis=1, keepdims=True)
                word_mass = jnp.exp2(lifted3 - word_top[:, None, :])
                patch_mass = jnp.exp2(lifted - patch_top).reshape(per, tokens, patch)
                word_sum = jnp.sum(word_mass, axis=1)
                patch_sum = jnp.sum(patch_mass, axis=2, keepdims=True)
                word_part = (0.5 / patch) / word_sum
                patch_part = (0.5 / tokens) / patch_sum
                blended = word_mass * word_part[:, None, :] + patch_mass * patch_part
                weights_out[i] = blended.reshape(lines, patch).astype(BF16)
                patch_logs = jnp.sum(
                    patch_top.reshape(per, tokens, 1) + jnp.log2(patch_sum), axis=1
                )
                scores_out[...] += place(i, word_top + jnp.log2(word_sum), patch_logs)
                return carry

            lax.fori_loop(0, per, image, 0)


def forward_call(offset, cands, counts, patches, words, prior):
    per, patch, width = patches.shape
    lines = per * words.shape[1]
    return pl.pallas_call(
        functools.partial(forward_kernel, offset),
        out_shape=(
            jax.ShapeDtypeStruct((per, lines, patch), BF16),
            jax.ShapeDtypeStruct((ROWS, LANES), F32),
        ),
        in_specs=[spec(pltpu.SMEM), spec(pltpu.SMEM), spec(), spec(), spec()],
        out_specs=(spec(), spec()),
        scratch_shapes=[pltpu.VMEM((1, patch), F32), pltpu.VMEM((1, patch), F32)],
        compiler_params=pltpu.CompilerParams(vmem_limit_bytes=VMEM_LIMIT),
        cost_estimate=pl.CostEstimate(
            flops=2 * per * lines * patch * width,
            bytes_accessed=2 * (per * patch * width + lines * width + per * lines * patch),
            transcendentals=per * lines * patch,
        ),
        name=f"forward_{offset}",
    )(cands, counts, patches, words, prior)


def stats_kernel(total, images, width, cands, counts, nse, *refs):
    tiles = refs[:total]
    coef_out, sums_out = refs[total:]
    row = lax.axis_index("img")
    me = lax.axis_index("cap")
    slots = cands.shape[2]
    per = images // (total * cands.shape[0])
    sub = lax.broadcasted_iota(jnp.int32, (ROWS, LANES), 0)
    lane = lax.broadcasted_iota(jnp.int32, (ROWS, LANES), 1)
    column = lane // per
    softness = jnp.exp(jnp.full((ROWS, LANES), nse[0], F32))
    kept, lives, marks = [], [], []
    peak = jnp.full((1, LANES), far_below, F32)
    for k in range(total):
        block = me ^ k
        live = jnp.zeros((ROWS, LANES), jnp.bool_)
        for s in range(slots):
            target = jnp.where(s < counts[row, block], cands[row, block, s], -1)
            live = live | (column == target)
        live = live & (sub < per)
        masked = jnp.where(live, tiles[k][...] * softness, far_below)
        kept.append(masked)
        lives.append(live)
        marks.append(live & (lane == block * per + sub))
        peak = jnp.maximum(peak, jnp.max(masked, axis=0, keepdims=True))
    mass = jnp.zeros((1, LANES), F32)
    for k in range(total):
        mass = mass + jnp.sum(
            jnp.where(lives[k], jnp.exp(kept[k] - peak), 0.0), axis=0, keepdims=True
        )
    col_ok = lane[:1] < total * per
    col_lse = jnp.where(col_ok, peak + jnp.log(jnp.where(col_ok, mass, 1.0)), 0.0)
    loss = jnp.zeros((ROWS, LANES), F32)
    temp = jnp.zeros((ROWS, LANES), F32)
    own = None
    for k in range(total):
        top = jnp.max(kept[k], axis=1, keepdims=True)
        part = jnp.sum(jnp.where(lives[k], jnp.exp(kept[k] - top), 0.0), axis=1, keepdims=True)
        row_lse = top + jnp.log(jnp.where(sub[:, :1] < per, part, 1.0))
        pull = jnp.where(
            lives[k],
            (0.5 / images)
            * (
                jnp.exp(kept[k] - row_lse)
                + jnp.exp(kept[k] - col_lse)
                - jnp.where(marks[k], 2.0, 0.0)
            ),
            0.0,
        )
        temp = temp + jnp.where(lives[k], pull * kept[k], 0.0)
        loss = loss + jnp.where((lane == 0) & (sub < per), row_lse, 0.0)
        loss = loss - jnp.where(marks[k], 2.0 * kept[k], 0.0)
        if k == 0:
            own = pull
    loss = loss + jnp.where(sub == 0, col_lse, 0.0)
    loss_total = jnp.sum(loss) * (0.5 / images)
    temp_total = jnp.sum(temp)
    sums_out[...] = jnp.where(sub == 0, loss_total, temp_total)
    factor = own * softness * (loss_scale * width**-0.5)
    for k in range(total):
        block = me ^ k
        spot = (lane == block * per + sub) & (sub < per)
        for i in range(per):
            line = jnp.broadcast_to(factor[i : i + 1], (ROWS, LANES))
            value = jnp.sum(jnp.where(spot, line, 0.0), axis=1, keepdims=True)
            coef_out[k, i] = jnp.broadcast_to(value, (ROWS, LANES))


def stats_call(images, width, cands, counts, nse, tiles, per):
    total = len(tiles)
    return pl.pallas_call(
        functools.partial(stats_kernel, total, images, width),
        out_shape=(
            jax.ShapeDtypeStruct((total, per, ROWS, LANES), F32),
            jax.ShapeDtypeStruct((ROWS, LANES), F32),
        ),
        in_specs=[spec(pltpu.SMEM)] * 3 + [spec()] * total,
        out_specs=(spec(), spec()),
        name="stats",
    )(cands, counts, nse, *tiles)


def scaled(weights, coef, i, per):
    lines, patch = weights.shape[1:]
    block = weights[i].astype(F32).reshape(per, lines // per, patch)
    factor = jnp.tile(coef[i, :per][:, None, :], (1, 1, patch // LANES))
    return (block * factor).reshape(lines, patch).astype(BF16)


def word_kernel(group, cands, counts, patches, coef, weights_a, weights_b, out_a, out_b):
    row = lax.axis_index("img")
    me = lax.axis_index("cap")
    per, patch, width = patches.shape
    for n, (weights, out) in enumerate(((weights_a, out_a), (weights_b, out_b))):
        offset = 2 * group + n
        live = block_is_live(cands, counts, row, me, me ^ offset, cands.shape[2])

        @pl.when(live)
        def _():
            total = jnp.zeros((weights.shape[1], width), F32)
            for i in range(per):
                total = total + lax.dot_general(
                    scaled(weights, coef.at[offset], i, per),
                    patches[i],
                    NN,
                    preferred_element_type=F32,
                )
            out[...] = total.reshape(out.shape).astype(out.dtype)

        @pl.when(jnp.logical_not(live))
        def _():
            out[...] = jnp.zeros(out.shape, out.dtype)


def word_call(group, cands, counts, patches, coef, weights_a, weights_b):
    per, patch, width = patches.shape
    lines = weights_a.shape[1]
    shape = (per, lines // per, width)
    return pl.pallas_call(
        functools.partial(word_kernel, group),
        out_shape=(jax.ShapeDtypeStruct(shape, F32), jax.ShapeDtypeStruct(shape, BF16)),
        in_specs=[spec(pltpu.SMEM)] * 2 + [spec()] * 4,
        out_specs=(spec(), spec()),
        compiler_params=pltpu.CompilerParams(vmem_limit_bytes=VMEM_LIMIT),
        cost_estimate=pl.CostEstimate(
            flops=4 * per * lines * patch * width,
            bytes_accessed=2 * per * patch * width + 4 * per * lines * patch + 6 * lines * width,
            transcendentals=0,
        ),
        name=f"word_{group}",
    )(cands, counts, patches, coef, weights_a, weights_b)


def patch_kernel(total, cands, counts, coef, *refs):
    weights, words, out, acc = refs[:total], refs[total : 2 * total], refs[-2], refs[-1]
    row = lax.axis_index("img")
    me = lax.axis_index("cap")
    per, patch, width = out.shape
    for k in range(total):

        def add(first):
            word_rows = words[k][...].reshape(weights[k].shape[1], width)
            for i in range(per):
                part = lax.dot_general(
                    scaled(weights[k], coef.at[k], i, per),
                    word_rows,
                    TN,
                    preferred_element_type=F32,
                )
                if first:
                    acc[i] = part
                else:
                    acc[i] += part

        if k == 0:
            add(True)
        else:
            live = block_is_live(cands, counts, row, me, me ^ k, cands.shape[2])
            pl.when(live)(functools.partial(add, False))
    out[...] = acc[...].astype(BF16)


def patch_call(cands, counts, coef, weights, words, shape):
    total = len(weights)
    per, patch, width = shape
    lines = weights[0].shape[1]
    return pl.pallas_call(
        functools.partial(patch_kernel, total),
        out_shape=jax.ShapeDtypeStruct(shape, BF16),
        in_specs=[spec(pltpu.SMEM)] * 2 + [spec()] * (1 + 2 * total),
        out_specs=spec(),
        scratch_shapes=[pltpu.VMEM(shape, F32)],
        compiler_params=pltpu.CompilerParams(vmem_limit_bytes=VMEM_LIMIT),
        cost_estimate=pl.CostEstimate(
            flops=2 * total * per * lines * patch * width,
            bytes_accessed=2 * total * (per * lines * patch + lines * width) + 2 * per * patch * width,
            transcendentals=0,
        ),
        name="patch",
    )(cands, counts, coef, *weights, *words)


def add_kernel(*refs):
    total = refs[0][...].astype(F32)
    for ref in refs[1:-1]:
        total = total + ref[...].astype(F32)
    refs[-1][...] = total.astype(refs[-1].dtype)


def add_call(name, dtype, *arrays):
    return pl.pallas_call(
        add_kernel,
        out_shape=jax.ShapeDtypeStruct(arrays[0].shape, dtype),
        in_specs=[spec()] * len(arrays),
        out_specs=spec(),
        name=name,
    )(*arrays)


def scalar_kernel(count, *refs):
    loss_out, temp_out = refs[count:]
    total = refs[0][...]
    for ref in refs[1:count]:
        total = total + ref[...]
    loss_out[0] = total[0, 0]
    temp_out[0] = total[1, 0]


def scalar_call(tiles):
    one = jax.ShapeDtypeStruct((1,), F32)
    return pl.pallas_call(
        functools.partial(scalar_kernel, len(tiles)),
        out_shape=(one, one),
        in_specs=[spec()] * len(tiles),
        out_specs=(spec(pltpu.SMEM), spec(pltpu.SMEM)),
        name="scalars",
    )(*tiles)


def body(patches, words, natural_sharpness_exponent, candidates, counts):
    total = lax.axis_size("cap")
    rows = lax.axis_size("img")
    per, patch, width = patches.shape
    images = per * total * rows
    groups = total // 2

    def hop(x, offset):
        return lax.ppermute(x, "cap", [(i, i ^ offset) for i in range(total)])

    words_at = [None] * total
    words_at[0] = words
    words_at[1] = hop(words, 1)
    for g in range(1, groups):
        words_at[2 * g] = hop(words, 2 * g)
    for g in range(1, groups):
        words_at[2 * g + 1] = hop(words_at[2 * g], 1)

    scores = jnp.zeros((ROWS, LANES), F32)
    weights = []
    for k in range(total):
        w, scores = forward_call(k, candidates, counts, patches, words_at[k], scores)
        weights.append(w)

    sibling = hop(scores, 1)
    pair = jnp.concatenate([scores, sibling], axis=0)
    tiles = [scores, sibling]
    for g in range(1, groups):
        other = hop(pair, 2 * g)
        tiles += [other[:ROWS], other[ROWS:]]
    coef, sums = stats_call(images, width, candidates, counts, natural_sharpness_exponent, tiles, per)

    sum_tiles = [sums]
    for k in range(1, rows):
        sum_tiles.append(lax.ppermute(sums, "img", [(i, (i + k) % rows) for i in range(rows)]))

    arrived = []
    kept = None
    for g in list(range(groups - 1, 0, -1)) + [0]:
        mine, theirs = word_call(
            g, candidates, counts, patches, coef, weights[2 * g], weights[2 * g + 1]
        )
        from_sibling = hop(theirs, 1)
        if g:
            joined = add_call(f"join_{g}", BF16, mine, from_sibling)
            arrived.append(hop(joined, 2 * g))
        else:
            kept = (mine, from_sibling)

    patch_grad = patch_call(candidates, counts, coef, weights, words_at, patches.shape)
    word_grad = add_call("finish", BF16, *kept, *arrived)
    loss, temp = scalar_call(sum_tiles)
    return patch_grad, word_grad, loss, temp


def solution(mesh):
    placed = (P(("img", "cap"), None, None), P(("img", "cap"), None, None), P(), P(), P())
    return jax.shard_map(
        body,
        mesh=mesh,
        in_specs=placed,
        out_specs=(P(("img", "cap"), None, None), P(("img", "cap"), None, None), P(), P()),
        check_vma=False,
    )
```

```python
import functools
import math

import jax
import jax.numpy as jnp
from jax import lax
from jax.experimental import pallas as pl
from jax.experimental.pallas import tpu as pltpu
from jax.sharding import PartitionSpec as P

sharpness = 4.0
loss_scale = 65536.0
far_below = -1e30
F32 = jnp.float32
BF16 = jnp.bfloat16
LANES = 128
ROWS = 8

NT = (((1,), (1,)), ((), ()))
NN = (((1,), (0,)), ((), ()))
TN = (((0,), (0,)), ((), ()))


def spec(space=pltpu.VMEM):
    return pl.BlockSpec(memory_space=space)


def near(*arrays):
    return tuple(pltpu.with_memory_space_constraint(x, pltpu.VMEM) for x in arrays)


def tiny():
    return pl.CostEstimate(flops=1, bytes_accessed=1, transcendentals=0)


def params(mib):
    return pltpu.CompilerParams(vmem_limit_bytes=mib << 20)


def fill_meta(cands, counts, nse, per, total, meta):
    row = lax.axis_index("img")
    me = lax.axis_index("cap")
    slots = cands.shape[0]
    sub = lax.broadcasted_iota(jnp.int32, (ROWS, LANES), 0)
    lane = lax.broadcasted_iota(jnp.int32, (ROWS, LANES), 1)
    column = lane // per
    first = sub < per
    for g in range(total // 2):
        even, odd = me ^ (2 * g), me ^ (2 * g + 1)
        live = jnp.zeros((ROWS, LANES), F32)
        for s in range(slots):
            here = jnp.where(s < counts[row, even], cands[s, row, even], -1)
            there = jnp.where(s < counts[row, odd], cands[s, row, odd], -1)
            live = jnp.where(column == jnp.where(first, here, there), 1.0, live)
        meta[g] = jnp.where(sub < 2 * per, live, 0.0)
    for part in range(total // ROWS):
        live = jnp.zeros((ROWS, LANES), F32)
        for s in range(slots):
            target = jnp.where(s < counts[row, me], cands[s, row, me], -1)
            live = jnp.where((me ^ (sub + ROWS * part)) == target, 1.0, live)
        meta[total // 2 + part] = live
    meta[meta.shape[0] - 1] = jnp.exp(jnp.full((ROWS, LANES), nse[0], F32))


def block_is_live(meta, total, offset):
    return meta[total // 2 + offset // ROWS, offset % ROWS, 0] > 0.0


def forward_kernel(offset, pieces, total, *refs):
    if offset:
        meta, patches, prior, *words = refs[: 3 + pieces]
    else:
        cands, counts, nse, patches, *words = refs[: 4 + pieces]
    weights_out, scores_out = refs[-4 - (not offset) :][:2]
    low, high = refs[-2:]
    me = lax.axis_index("cap")
    column = me ^ offset
    per, patch, width = patches.shape
    tokens = words[0].shape[1]
    lines = per * tokens
    scale = sharpness * width**-0.5 * math.log2(math.e)

    def start():
        scores_out[...] = prior[...] if offset else jnp.zeros(scores_out.shape, F32)

    start()
    if not offset:
        fill_meta(cands, counts, nse, per, total, refs[-3])

    def score():
        sub = lax.broadcasted_iota(jnp.int32, (ROWS, LANES), 0)
        lane = lax.broadcasted_iota(jnp.int32, (ROWS, LANES), 1)
        spot = lane == column * per + sub

        def place(i, over_words, over_patches):
            part = jnp.sum(over_words, axis=1, keepdims=True) * (1.0 / patch)
            part = part + over_patches * (1.0 / tokens)
            part = part * (0.5 * math.log(2.0) / sharpness)
            part = jnp.concatenate([part, jnp.zeros((ROWS - per, 1), F32)], axis=0)
            line = jnp.sum(jnp.where(spot & (sub < per), part, 0.0), axis=0, keepdims=True)
            return jnp.where(sub == i, line, 0.0)

        word_rows = jnp.concatenate(
            [w[...].reshape(w.shape[0] * tokens, width) for w in words], axis=0
        )
        low[...] = jnp.full(low.shape, 1.0, F32)
        high[...] = jnp.full(high.shape, 1.0, F32)
        tile = jnp.zeros((ROWS, LANES), F32)
        for i in range(per):
            raw = lax.dot_general(word_rows, patches[i], NT, preferred_element_type=F32)
            mass = jnp.exp2(raw * scale)
            mass3 = mass.reshape(per, tokens, patch)
            word_sum = jnp.sum(mass3, axis=1)
            patch_sum = jnp.sum(mass, axis=1, keepdims=True)
            low[...] = jnp.minimum(low[...], jnp.min(word_sum, axis=0, keepdims=True))
            high[...] = jnp.maximum(high[...], jnp.max(word_sum, axis=0, keepdims=True))
            low[...] = jnp.minimum(low[...], jnp.min(patch_sum, axis=0, keepdims=True))
            high[...] = jnp.maximum(high[...], jnp.max(patch_sum, axis=0, keepdims=True))
            word_part = (0.5 / patch) / word_sum
            patch_part = (0.5 / tokens) / patch_sum
            blended = mass3 * (word_part[:, None, :] + patch_part.reshape(per, tokens, 1))
            weights_out[i] = blended.reshape(lines, patch).astype(BF16)
            patch_logs = jnp.sum(jnp.log2(patch_sum).reshape(per, tokens, 1), axis=1)
            tile = tile + place(i, jnp.log2(word_sum), patch_logs)
        scores_out[...] += tile
        safe = (jnp.min(low[...]) > 2.0**-90) & (jnp.max(high[...]) < 2.0**120)

        @pl.when(jnp.logical_not(safe))
        def _():
            start()

            def image(i, carry):
                raw = lax.dot_general(word_rows, patches[i], NT, preferred_element_type=F32)
                lifted = raw * scale
                lifted3 = lifted.reshape(per, tokens, patch)
                word_top = jnp.max(lifted3, axis=1)
                patch_top = jnp.max(lifted, axis=1, keepdims=True)
                word_mass = jnp.exp2(lifted3 - word_top[:, None, :])
                patch_mass = jnp.exp2(lifted - patch_top).reshape(per, tokens, patch)
                word_sum = jnp.sum(word_mass, axis=1)
                patch_sum = jnp.sum(patch_mass, axis=2, keepdims=True)
                word_part = (0.5 / patch) / word_sum
                patch_part = (0.5 / tokens) / patch_sum
                blended = word_mass * word_part[:, None, :] + patch_mass * patch_part
                weights_out[i] = blended.reshape(lines, patch).astype(BF16)
                patch_logs = jnp.sum(
                    patch_top.reshape(per, tokens, 1) + jnp.log2(patch_sum), axis=1
                )
                scores_out[...] += place(i, word_top + jnp.log2(word_sum), patch_logs)
                return carry

            lax.fori_loop(0, per, image, 0)

    if offset:
        pl.when(block_is_live(meta, total, offset))(score)
    else:
        score()


def forward_call(offset, total, patches, words, extra):
    per, patch, width = patches.shape
    lines = per * words[0].shape[1]
    shapes = (pltpu.VMEM((per, lines, patch), BF16), pltpu.VMEM((ROWS, LANES), F32))
    if offset:
        meta, prior = extra
        args = near(meta, patches, prior, *words)
        specs = [spec()] * len(args)
    else:
        args = (*extra, *near(patches, *words))
        specs = [spec(pltpu.SMEM)] * 3 + [spec()] * (len(args) - 3)
        shapes += (pltpu.VMEM((total // 2 + total // ROWS + 1, ROWS, LANES), F32),)
    return pl.pallas_call(
        functools.partial(forward_kernel, offset, len(words), total),
        out_shape=shapes,
        in_specs=specs,
        out_specs=(spec(),) * len(shapes),
        scratch_shapes=[pltpu.VMEM((1, patch), F32), pltpu.VMEM((1, patch), F32)],
        compiler_params=params(12),
        cost_estimate=tiny(),
        name=f"forward_{offset}",
    )(*args)


def stats_kernel(total, images, per, width, meta, *refs):
    tiles = refs[: total // 2]
    coef_out, sums_out = refs[total // 2 :]
    me = lax.axis_index("cap")
    sub = lax.broadcasted_iota(jnp.int32, (ROWS, LANES), 0)
    lane = lax.broadcasted_iota(jnp.int32, (ROWS, LANES), 1)
    first = sub < per
    image = jnp.where(first, sub, sub - per)
    softness = meta[meta.shape[0] - 1]
    kept, lives, marks = [], [], []
    peak = jnp.full((1, LANES), far_below, F32)
    for g in range(total // 2):
        even, odd = me ^ (2 * g), me ^ (2 * g + 1)
        live = meta[g] > 0.0
        masked = jnp.where(live, tiles[g][...] * softness, far_below)
        kept.append(masked)
        lives.append(live)
        marks.append(live & (lane == jnp.where(first, even, odd) * per + image))
        peak = jnp.maximum(peak, jnp.max(masked, axis=0, keepdims=True))
    mass = jnp.zeros((1, LANES), F32)
    for masked, live in zip(kept, lives):
        mass = mass + jnp.sum(
            jnp.where(live, jnp.exp(masked - peak), 0.0), axis=0, keepdims=True
        )
    col_ok = lane[:1] < total * per
    col_lse = jnp.where(col_ok, peak + jnp.log(jnp.where(col_ok, mass, 1.0)), 0.0)
    loss = jnp.where(sub == 0, col_lse, 0.0)
    temp = jnp.zeros((ROWS, LANES), F32)
    pulls = []
    for masked, live, mark in zip(kept, lives, marks):
        top = jnp.max(masked, axis=1, keepdims=True)
        part = jnp.sum(jnp.where(live, jnp.exp(masked - top), 0.0), axis=1, keepdims=True)
        row_lse = top + jnp.log(jnp.where(sub[:, :1] < 2 * per, part, 1.0))
        pull = jnp.where(
            live,
            (0.5 / images)
            * (jnp.exp(masked - row_lse) + jnp.exp(masked - col_lse) - jnp.where(mark, 2.0, 0.0)),
            0.0,
        )
        pulls.append(pull)
        temp = temp + jnp.where(live, pull * masked, 0.0)
        loss = loss + jnp.where((lane == 0) & (sub < 2 * per), row_lse, 0.0)
        loss = loss - jnp.where(mark, 2.0 * masked, 0.0)
    loss_total = jnp.sum(loss) * (0.5 / images)
    temp_total = jnp.sum(temp)
    sums_out[...] = jnp.where(sub == 0, loss_total, temp_total)
    factor = pulls[0] * softness * (loss_scale * width**-0.5)
    for k in range(total):
        spot = (lane == (me ^ k) * per + sub) & first
        for i in range(per):
            line = jnp.broadcast_to(factor[i : i + 1], (ROWS, LANES))
            value = jnp.sum(jnp.where(spot, line, 0.0), axis=1, keepdims=True)
            coef_out[k, i] = jnp.broadcast_to(value, (ROWS, LANES))


def stats_call(images, per, width, meta, tiles):
    total = 2 * len(tiles)
    return pl.pallas_call(
        functools.partial(stats_kernel, total, images, per, width),
        out_shape=(
            pltpu.VMEM((total, per, ROWS, LANES), F32),
            pltpu.VMEM((ROWS, LANES), F32),
        ),
        in_specs=[spec()] * (1 + len(tiles)),
        out_specs=(spec(), spec()),
        compiler_params=params(4),
        cost_estimate=tiny(),
        name="stats",
    )(*near(meta, *tiles))


def pair_kernel(per, own, other, out):
    sub = lax.broadcasted_iota(jnp.int32, (ROWS, LANES), 0)
    moved = jnp.concatenate([other[...]] * 2, axis=0)[ROWS - per : 2 * ROWS - per]
    out[...] = jnp.where(sub < per, own[...], moved)


def pair_call(per, own, other):
    return pl.pallas_call(
        functools.partial(pair_kernel, per),
        out_shape=pltpu.VMEM((ROWS, LANES), F32),
        in_specs=[spec()] * 2,
        out_specs=spec(),
        compiler_params=params(4),
        cost_estimate=tiny(),
        name="pair",
    )(*near(own, other))


def scaled(weights, coef, i, per):
    lines, patch = weights.shape[1:]
    block = weights[i].astype(F32).reshape(per, lines // per, patch)
    factor = jnp.tile(coef[i, :per][:, None, :], (1, 1, patch // LANES))
    return (block * factor).reshape(lines, patch).astype(BF16)


def word_kernel(group, total, meta, patches, coef, weights_a, weights_b, low_out, high_out, out_b):
    per, patch, width = patches.shape
    half = low_out.shape[0]
    for n, weights in enumerate((weights_a, weights_b)):
        offset = 2 * group + n
        shape = (per, weights.shape[1] // per, width)

        def put(value):
            if n:
                out_b[...] = value.astype(out_b.dtype)
            else:
                low_out[...] = value[:half]
                high_out[...] = value[half:]

        def run():
            wide = jnp.concatenate(
                [scaled(weights, coef.at[offset], i, per) for i in range(per)], axis=1
            )
            rows = patches[...].reshape(per * patch, width)
            put(lax.dot_general(wide, rows, NN, preferred_element_type=F32).reshape(shape))

        if offset:
            live = block_is_live(meta, total, offset)
            pl.when(live)(run)
            pl.when(jnp.logical_not(live))(lambda: put(jnp.zeros(shape, F32)))
        else:
            run()


def word_call(group, total, meta, patches, coef, weights_a, weights_b):
    per, patch, width = patches.shape
    shape = (per, weights_a.shape[1] // per, width)
    part = (per // 2, *shape[1:])
    return pl.pallas_call(
        functools.partial(word_kernel, group, total),
        out_shape=(pltpu.VMEM(part, F32), pltpu.VMEM(part, F32), pltpu.VMEM(shape, BF16)),
        in_specs=[spec()] * 5,
        out_specs=(spec(),) * 3,
        compiler_params=params(12),
        cost_estimate=tiny(),
        name=f"word_{group}",
    )(*near(meta, patches, coef, weights_a, weights_b))


def patch_kernel(total, split, meta, coef, *refs):
    weights, words, out, acc = refs[:total], refs[total:-2], refs[-2], refs[-1]
    per, patch, width = out.shape
    for k in range(total):
        pieces, words = words[: split[k]], words[split[k] :]

        def add(k=k, pieces=pieces):
            word_rows = jnp.concatenate(
                [w[...].reshape(w.shape[0] * w.shape[1], width) for w in pieces], axis=0
            )
            for i in range(per):
                part = lax.dot_general(
                    scaled(weights[k], coef.at[k], i, per),
                    word_rows,
                    TN,
                    preferred_element_type=F32,
                )
                if k:
                    acc[i] += part
                else:
                    acc[i] = part

        if k:
            pl.when(block_is_live(meta, total, k))(add)
        else:
            add()
    out[...] = acc[...].astype(BF16)


def patch_call(meta, coef, weights, words, shape):
    total = len(weights)
    flat = [piece for pieces in words for piece in pieces]
    return pl.pallas_call(
        functools.partial(patch_kernel, total, tuple(len(p) for p in words)),
        out_shape=jax.ShapeDtypeStruct(shape, BF16),
        in_specs=[spec()] * (2 + total + len(flat)),
        out_specs=spec(),
        scratch_shapes=[pltpu.VMEM(shape, F32)],
        compiler_params=params(16),
        cost_estimate=tiny(),
        name="patch",
    )(*near(meta, coef, *weights, *flat))


def half_kernel(start, x, out):
    out[...] = x[start : start + out.shape[0]]


def half_call(start, x):
    count = x.shape[0] // 2
    return pl.pallas_call(
        functools.partial(half_kernel, start),
        out_shape=pltpu.VMEM((count, *x.shape[1:]), x.dtype),
        in_specs=[spec()],
        out_specs=spec(),
        compiler_params=params(4),
        cost_estimate=tiny(),
        name=f"half_{start}",
    )(*near(x))


def join_kernel(low, high, sibling, low_out, high_out):
    half = low.shape[0]
    low_out[...] = (low[...] + sibling[:half].astype(F32)).astype(low_out.dtype)
    high_out[...] = (high[...] + sibling[half:].astype(F32)).astype(high_out.dtype)


def join_call(name, low, high, sibling, low_type, high_type):
    return pl.pallas_call(
        join_kernel,
        out_shape=(pltpu.VMEM(low.shape, low_type), pltpu.VMEM(high.shape, high_type)),
        in_specs=[spec()] * 3,
        out_specs=(spec(),) * 2,
        compiler_params=params(4),
        cost_estimate=tiny(),
        name=name,
    )(*near(low, high, sibling))


def add_kernel(*refs):
    total = refs[0][...].astype(F32)
    for ref in refs[1:-1]:
        total = total + ref[...].astype(F32)
    refs[-1][...] = total.astype(refs[-1].dtype)


def add_call(name, dtype, *arrays):
    return pl.pallas_call(
        add_kernel,
        out_shape=pltpu.VMEM(arrays[0].shape, dtype),
        in_specs=[spec()] * len(arrays),
        out_specs=spec(),
        compiler_params=params(4),
        cost_estimate=tiny(),
        name=name,
    )(*near(*arrays))


def finish_kernel(count, *refs):
    out = refs[-1]
    half = out.shape[0] // 2
    for n, part in enumerate((refs[:count], refs[count:-1])):
        total = part[0][...]
        for ref in part[1:]:
            total = total + ref[...].astype(F32)
        out[half * n : half * (n + 1)] = total.astype(BF16)


def finish_call(lows, highs, shape):
    return pl.pallas_call(
        functools.partial(finish_kernel, len(lows)),
        out_shape=jax.ShapeDtypeStruct(shape, BF16),
        in_specs=[spec()] * (len(lows) + len(highs)),
        out_specs=spec(),
        compiler_params=params(8),
        cost_estimate=tiny(),
        name="finish",
    )(*near(*lows, *highs))


def scalar_kernel(mine, other, loss_out, temp_out):
    total = mine[...] + other[...]
    loss_out[0] = total[0, 0]
    temp_out[0] = total[1, 0]


def scalar_call(mine, other):
    one = jax.ShapeDtypeStruct((1,), F32)
    return pl.pallas_call(
        scalar_kernel,
        out_shape=(one, one),
        in_specs=[spec()] * 2,
        out_specs=(spec(pltpu.SMEM), spec(pltpu.SMEM)),
        compiler_params=params(4),
        cost_estimate=tiny(),
        name="scalars",
    )(*near(mine, other))


def body(patches, words, natural_sharpness_exponent, candidates, counts):
    total = lax.axis_size("cap")
    rows = lax.axis_size("img")
    per, patch, width = patches.shape
    images = per * total * rows
    groups = total // 2
    half = per // 2
    bits = [1 << n for n in range(groups.bit_length() - 1)]
    barrier = lax.optimization_barrier

    def low_bit(g):
        return g & -g

    def high_bit(g):
        return 1 << (g.bit_length() - 1)

    def hop(x, offset):
        return lax.ppermute(x, "cap", [(i, i ^ offset) for i in range(total)])

    words_at = [None] * total
    words_at[0] = (words,)
    for b in bits:
        words_at[2 * b] = (hop(words, 2 * b),)
    words_at[1] = (hop(words, 1),)

    meta = None
    weights, scores = [], []

    def forward(k):
        nonlocal meta
        if k:
            extra = (meta, scores[-1])
        else:
            extra = (jnp.transpose(candidates, (2, 0, 1)), counts, natural_sharpness_exponent)
        made = forward_call(k, total, patches, words_at[k], extra)
        if not k:
            meta = made[2]
        weights.append(made[0])
        scores.append(made[1])

    forward(0)
    forward(1)
    direct = [words_at[2 * b][0] for b in bits]
    *direct, _ = barrier((*direct, scores[-1]))
    for b, x in zip(bits, direct):
        words_at[2 * b] = (x,)

    def part(g, side):
        pieces = words_at[2 * g]
        return pieces[side] if len(pieces) == 2 else half_call(side * half, pieces[0])

    for g in range(1, groups):
        if words_at[2 * g] is None:
            words_at[2 * g] = (
                hop(part(g ^ high_bit(g), 0), 2 * high_bit(g)),
                hop(part(g ^ low_bit(g), 1), 2 * low_bit(g)),
            )
    for b in bits:
        words_at[2 * b + 1] = (hop(words_at[2 * b][0], 1),)
    sequence = bits + [g for g in range(1, groups) if g not in bits]
    order = [0, 1] + [2 * g + n for g in sequence for n in (0, 1)]
    done = 2
    for g in sequence:
        if words_at[2 * g + 1] is None:
            *pieces, _ = barrier((*words_at[2 * g], scores[-2]))
            words_at[2 * g] = tuple(pieces)
            words_at[2 * g + 1] = tuple(hop(x, 1) for x in pieces)
        forward(2 * g)
        forward(2 * g + 1)
    by_offset = dict(zip(order, weights))
    weights = [by_offset[k] for k in range(total)]
    scores = scores[-1]

    pair = pair_call(per, scores, hop(scores, 1))
    tiles = [pair] + [hop(pair, 2 * g) for g in range(1, groups)]
    coef, sums = stats_call(images, per, width, meta, tiles)

    lows = [[] for _ in range(groups)]
    highs = [[] for _ in range(groups)]
    top = bits[-1] if bits else 0
    order = sorted(range(1, groups), key=lambda g: -bin(g).count("1")) + [0]
    waiting = []

    def settle(g, low, high, sibling):
        low, high = join_call(
            f"join_{g}",
            low,
            high,
            sibling,
            BF16 if g & 1 else F32,
            BF16 if g & top else F32,
        )
        lows[g].append(low)
        highs[g].append(high)
        return low

    def send(side, g, b):
        store = (lows, highs)[side]
        terms = store[g]
        value = terms[0] if len(terms) == 1 else add_call(f"mix_{side}_{g}", BF16, *terms)
        store[g ^ b].append(hop(value, 2 * b))

    word_coef = coef
    for g in order:
        low, high, theirs = word_call(
            g, total, meta, patches, word_coef, weights[2 * g], weights[2 * g + 1]
        )
        sibling = hop(theirs, 1)
        if waiting:
            joined = settle(*waiting.pop())
            word_coef, _ = barrier((word_coef, joined))
        waiting.append((g, low, high, sibling))
    settle(*waiting.pop())
    for b in bits:
        for g in sorted(range(1, groups), reverse=True):
            if low_bit(g) == b:
                send(0, g, b)
    for b in reversed(bits):
        for g in sorted(range(1, groups), reverse=True):
            if high_bit(g) == b:
                send(1, g, b)

    step = 1
    while 2 * step < rows:
        other = lax.ppermute(sums, "img", [(i, i ^ step) for i in range(rows)])
        sums = add_call(f"sums_{step}", F32, sums, other)
        step *= 2
    other = lax.ppermute(sums, "img", [(i, i ^ step) for i in range(rows)])
    loss, temp = scalar_call(sums, other)

    patch_grad = patch_call(meta, coef, weights, words_at, patches.shape)
    word_grad = finish_call(lows[0], highs[0], words.shape)
    return patch_grad, word_grad, loss, temp


def solution(mesh):
    placed = (P(("img", "cap"), None, None), P(("img", "cap"), None, None), P(), P(), P())
    return jax.shard_map(
        body,
        mesh=mesh,
        in_specs=placed,
        out_specs=(P(("img", "cap"), None, None), P(("img", "cap"), None, None), P(), P()),
        check_vma=False,
    )
```

```python
import functools
import math

import jax
import jax.numpy as jnp
from jax import lax
from jax.experimental import pallas as pl
from jax.experimental.pallas import tpu as pltpu
from jax.sharding import PartitionSpec as P

sharpness = 4.0
loss_scale = 65536.0
far_below = -1e30
F32 = jnp.float32
BF16 = jnp.bfloat16
LANES = 128
ROWS = 8

NT = (((1,), (1,)), ((), ()))
NN = (((1,), (0,)), ((), ()))
TN = (((0,), (0,)), ((), ()))


def spec(space=pltpu.VMEM):
    return pl.BlockSpec(memory_space=space)


def near(*arrays):
    return tuple(pltpu.with_memory_space_constraint(x, pltpu.VMEM) for x in arrays)


def tiny():
    return pl.CostEstimate(flops=1, bytes_accessed=1, transcendentals=0)


def params(mib):
    return pltpu.CompilerParams(vmem_limit_bytes=mib << 20)


def fill_meta(cands, counts, nse, per, total, meta):
    row = lax.axis_index("img")
    me = lax.axis_index("cap")
    slots = cands.shape[0]
    sub = lax.broadcasted_iota(jnp.int32, (ROWS, LANES), 0)
    lane = lax.broadcasted_iota(jnp.int32, (ROWS, LANES), 1)
    column = lane // per
    first = sub < per
    for g in range(total // 2):
        even, odd = me ^ (2 * g), me ^ (2 * g + 1)
        live = jnp.zeros((ROWS, LANES), F32)
        for s in range(slots):
            here = jnp.where(s < counts[row, even], cands[s, row, even], -1)
            there = jnp.where(s < counts[row, odd], cands[s, row, odd], -1)
            live = jnp.where(column == jnp.where(first, here, there), 1.0, live)
        meta[g] = jnp.where(sub < 2 * per, live, 0.0)
    for part in range(total // ROWS):
        live = jnp.zeros((ROWS, LANES), F32)
        for s in range(slots):
            target = jnp.where(s < counts[row, me], cands[s, row, me], -1)
            live = jnp.where((me ^ (sub + ROWS * part)) == target, 1.0, live)
        meta[total // 2 + part] = live
    meta[meta.shape[0] - 1] = jnp.exp(jnp.full((ROWS, LANES), nse[0], F32))


def block_is_live(meta, total, offset):
    return meta[total // 2 + offset // ROWS, offset % ROWS, 0] > 0.0


def forward_kernel(offset, pieces, total, product, *refs):
    if offset:
        meta, patches, prior, *words = refs[: 3 + pieces]
    else:
        cands, counts, nse, patches, *words = refs[: 4 + pieces]
    outs = list(refs[(3 if offset else 4) + pieces : -2])
    weights_out, scores_out = outs[:2]
    low, high = refs[-2:]
    me = lax.axis_index("cap")
    column = me ^ offset
    per, patch, width = patches.shape
    tokens = words[0].shape[1]
    lines = per * tokens
    scale = sharpness * width**-0.5 * math.log2(math.e)

    def start():
        scores_out[...] = prior[...] if offset else jnp.zeros(scores_out.shape, F32)

    start()
    if not offset:
        fill_meta(cands, counts, nse, per, total, outs[-1])

    def score():
        sub = lax.broadcasted_iota(jnp.int32, (ROWS, LANES), 0)
        lane = lax.broadcasted_iota(jnp.int32, (ROWS, LANES), 1)
        spot = lane == column * per + sub

        def place(i, over_words, over_patches):
            part = jnp.sum(over_words, axis=1, keepdims=True) * (1.0 / patch)
            part = part + over_patches * (1.0 / tokens)
            part = part * (0.5 * math.log(2.0) / sharpness)
            part = jnp.concatenate([part, jnp.zeros((ROWS - per, 1), F32)], axis=0)
            line = jnp.sum(jnp.where(spot & (sub < per), part, 0.0), axis=0, keepdims=True)
            return jnp.where(sub == i, line, 0.0)

        word_rows = jnp.concatenate(
            [w[...].reshape(w.shape[0] * tokens, width) for w in words], axis=0
        )
        low[...] = jnp.full(low.shape, 1.0, F32)
        high[...] = jnp.full(high.shape, 1.0, F32)
        tile = jnp.zeros((ROWS, LANES), F32)
        for i in range(per):
            raw = lax.dot_general(word_rows, patches[i], NT, preferred_element_type=F32)
            mass = jnp.exp2(raw * scale)
            mass3 = mass.reshape(per, tokens, patch)
            word_sum = jnp.sum(mass3, axis=1)
            patch_sum = jnp.sum(mass, axis=1, keepdims=True)
            low[...] = jnp.minimum(low[...], jnp.min(word_sum, axis=0, keepdims=True))
            high[...] = jnp.maximum(high[...], jnp.max(word_sum, axis=0, keepdims=True))
            low[...] = jnp.minimum(low[...], jnp.min(patch_sum, axis=0, keepdims=True))
            high[...] = jnp.maximum(high[...], jnp.max(patch_sum, axis=0, keepdims=True))
            word_part = (0.5 / patch) / word_sum
            patch_part = (0.5 / tokens) / patch_sum
            blended = mass3 * (word_part[:, None, :] + patch_part.reshape(per, tokens, 1))
            weights_out[i] = blended.reshape(lines, patch).astype(BF16)
            patch_logs = jnp.sum(jnp.log2(patch_sum).reshape(per, tokens, 1), axis=1)
            tile = tile + place(i, jnp.log2(word_sum), patch_logs)
        scores_out[...] += tile
        safe = (jnp.min(low[...]) > 2.0**-90) & (jnp.max(high[...]) < 2.0**120)

        @pl.when(jnp.logical_not(safe))
        def _():
            start()

            def image(i, carry):
                raw = lax.dot_general(word_rows, patches[i], NT, preferred_element_type=F32)
                lifted = raw * scale
                lifted3 = lifted.reshape(per, tokens, patch)
                word_top = jnp.max(lifted3, axis=1)
                patch_top = jnp.max(lifted, axis=1, keepdims=True)
                word_mass = jnp.exp2(lifted3 - word_top[:, None, :])
                patch_mass = jnp.exp2(lifted - patch_top).reshape(per, tokens, patch)
                word_sum = jnp.sum(word_mass, axis=1)
                patch_sum = jnp.sum(patch_mass, axis=2, keepdims=True)
                word_part = (0.5 / patch) / word_sum
                patch_part = (0.5 / tokens) / patch_sum
                blended = word_mass * word_part[:, None, :] + patch_mass * patch_part
                weights_out[i] = blended.reshape(lines, patch).astype(BF16)
                patch_logs = jnp.sum(
                    patch_top.reshape(per, tokens, 1) + jnp.log2(patch_sum), axis=1
                )
                scores_out[...] += place(i, word_top + jnp.log2(word_sum), patch_logs)
                return carry

            lax.fori_loop(0, per, image, 0)

        if product:
            for i in range(per):
                outs[2][i] = lax.dot_general(
                    weights_out[i], patches[i], NN, preferred_element_type=F32
                )

    if offset:
        live = block_is_live(meta, total, offset)
        pl.when(live)(score)

        @pl.when(jnp.logical_not(live))
        def _():
            weights_out[...] = jnp.zeros(weights_out.shape, weights_out.dtype)

    else:
        score()


def forward_call(offset, total, product, patches, words, extra):
    per, patch, width = patches.shape
    lines = per * words[0].shape[1]
    shapes = (pltpu.VMEM((per, lines, patch), BF16), pltpu.VMEM((ROWS, LANES), F32))
    if product:
        shapes += (pltpu.VMEM((per, lines, width), F32),)
    if offset:
        meta, prior = extra
        args = near(meta, patches, prior, *words)
        specs = [spec()] * len(args)
    else:
        args = (*extra, *near(patches, *words))
        specs = [spec(pltpu.SMEM)] * 3 + [spec()] * (len(args) - 3)
        shapes += (pltpu.VMEM((total // 2 + total // ROWS + 1, ROWS, LANES), F32),)
    return pl.pallas_call(
        functools.partial(forward_kernel, offset, len(words), total, product),
        out_shape=shapes,
        in_specs=specs,
        out_specs=(spec(),) * len(shapes),
        scratch_shapes=[pltpu.VMEM((1, patch), F32), pltpu.VMEM((1, patch), F32)],
        compiler_params=params(12),
        cost_estimate=tiny(),
        name=f"forward_{offset}",
    )(*args)


def stats_kernel(total, images, per, width, meta, *refs):
    tiles = refs[: total // 2]
    coef_out, sums_out = refs[total // 2 :]
    me = lax.axis_index("cap")
    sub = lax.broadcasted_iota(jnp.int32, (ROWS, LANES), 0)
    lane = lax.broadcasted_iota(jnp.int32, (ROWS, LANES), 1)
    first = sub < per
    image = jnp.where(first, sub, sub - per)
    softness = meta[meta.shape[0] - 1]
    kept, lives, marks = [], [], []
    peak = jnp.full((1, LANES), far_below, F32)
    for g in range(total // 2):
        even, odd = me ^ (2 * g), me ^ (2 * g + 1)
        live = meta[g] > 0.0
        masked = jnp.where(live, tiles[g][...] * softness, far_below)
        kept.append(masked)
        lives.append(live)
        marks.append(live & (lane == jnp.where(first, even, odd) * per + image))
        peak = jnp.maximum(peak, jnp.max(masked, axis=0, keepdims=True))
    mass = jnp.zeros((1, LANES), F32)
    for masked, live in zip(kept, lives):
        mass = mass + jnp.sum(
            jnp.where(live, jnp.exp(masked - peak), 0.0), axis=0, keepdims=True
        )
    col_ok = lane[:1] < total * per
    col_lse = jnp.where(col_ok, peak + jnp.log(jnp.where(col_ok, mass, 1.0)), 0.0)
    loss = jnp.where(sub == 0, col_lse, 0.0)
    temp = jnp.zeros((ROWS, LANES), F32)
    pulls = []
    for masked, live, mark in zip(kept, lives, marks):
        top = jnp.max(masked, axis=1, keepdims=True)
        part = jnp.sum(jnp.where(live, jnp.exp(masked - top), 0.0), axis=1, keepdims=True)
        row_lse = top + jnp.log(jnp.where(sub[:, :1] < 2 * per, part, 1.0))
        pull = jnp.where(
            live,
            (0.5 / images)
            * (jnp.exp(masked - row_lse) + jnp.exp(masked - col_lse) - jnp.where(mark, 2.0, 0.0)),
            0.0,
        )
        pulls.append(pull)
        temp = temp + jnp.where(live, pull * masked, 0.0)
        loss = loss + jnp.where((lane == 0) & (sub < 2 * per), row_lse, 0.0)
        loss = loss - jnp.where(mark, 2.0 * masked, 0.0)
    loss_total = jnp.sum(loss) * (0.5 / images)
    temp_total = jnp.sum(temp)
    sums_out[...] = jnp.where(sub == 0, loss_total, temp_total)
    factor = pulls[0] * softness * (loss_scale * width**-0.5)
    for k in range(total):
        spot = (lane == (me ^ k) * per + sub) & first
        for i in range(per):
            line = jnp.broadcast_to(factor[i : i + 1], (ROWS, LANES))
            value = jnp.sum(jnp.where(spot, line, 0.0), axis=1, keepdims=True)
            coef_out[k, i] = jnp.broadcast_to(value, (ROWS, LANES))


def stats_call(images, per, width, meta, tiles):
    total = 2 * len(tiles)
    return pl.pallas_call(
        functools.partial(stats_kernel, total, images, per, width),
        out_shape=(
            pltpu.VMEM((total, per, ROWS, LANES), F32),
            pltpu.VMEM((ROWS, LANES), F32),
        ),
        in_specs=[spec()] * (1 + len(tiles)),
        out_specs=(spec(), spec()),
        compiler_params=params(4),
        cost_estimate=tiny(),
        name="stats",
    )(*near(meta, *tiles))


def pair_kernel(per, own, other, out):
    sub = lax.broadcasted_iota(jnp.int32, (ROWS, LANES), 0)
    moved = jnp.concatenate([other[...]] * 2, axis=0)[ROWS - per : 2 * ROWS - per]
    out[...] = jnp.where(sub < per, own[...], moved)


def pair_call(per, own, other):
    return pl.pallas_call(
        functools.partial(pair_kernel, per),
        out_shape=pltpu.VMEM((ROWS, LANES), F32),
        in_specs=[spec()] * 2,
        out_specs=spec(),
        compiler_params=params(4),
        cost_estimate=tiny(),
        name="pair",
    )(*near(own, other))


def scaled(weights, coef, i, per):
    lines, patch = weights.shape[1:]
    block = weights[i].astype(F32).reshape(per, lines // per, patch)
    factor = jnp.tile(coef[i, :per][:, None, :], (1, 1, patch // LANES))
    return (block * factor).reshape(lines, patch).astype(BF16)


def word_kernel(group, total, patches, meta, coef, source_a, source_b, low_out, high_out, out_b):
    half, tokens, width = low_out.shape
    per = 2 * half
    for n, source in enumerate((source_a, source_b)):
        offset = 2 * group + n
        shape = (per, tokens, width)

        def put(value):
            if n:
                out_b[...] = value.astype(out_b.dtype)
            else:
                low_out[...] = value[:half]
                high_out[...] = value[half:]

        def run():
            if patches is None:
                value = jnp.zeros(shape, F32)
                for i in range(per):
                    factor = jnp.tile(coef[offset, i, :per][:, None, :], (1, 1, width // LANES))
                    value = value + source[i].reshape(shape) * factor
                put(value)
                return
            wide = jnp.concatenate(
                [scaled(source, coef.at[offset], i, per) for i in range(per)], axis=1
            )
            rows = patches[...].reshape(-1, width)
            put(lax.dot_general(wide, rows, NN, preferred_element_type=F32).reshape(shape))

        if offset:
            live = block_is_live(meta, total, offset)
            pl.when(live)(run)
            pl.when(jnp.logical_not(live))(lambda: put(jnp.zeros(shape, F32)))
        else:
            run()


def word_products(group, total, meta, coef, *refs):
    word_kernel(group, total, None, meta, coef, *refs)


def word_blends(group, total, patches, meta, coef, *refs):
    word_kernel(group, total, patches, meta, coef, *refs)


def word_call(group, total, shape, meta, coef, source_a, source_b, patches=()):
    part = (shape[0] // 2, *shape[1:])
    return pl.pallas_call(
        functools.partial(word_blends if patches else word_products, group, total),
        out_shape=(pltpu.VMEM(part, F32), pltpu.VMEM(part, F32), pltpu.VMEM(shape, BF16)),
        in_specs=[spec()] * (4 + len(patches)),
        out_specs=(spec(),) * 3,
        compiler_params=params(12),
        cost_estimate=tiny(),
        name=f"word_{group}",
    )(*near(*patches, meta, coef, source_a, source_b))


def patch_kernel(total, start, split, coef, *refs):
    out, result, sems = refs[-3:]
    weights, words = refs[:total], refs[total : total + sum(split)]
    count, patch, width = result.shape
    per = out.shape[0]

    def save(i):
        return pltpu.make_async_copy(result.at[i], out.at[start + i], sems.at[i])

    word_rows = jnp.concatenate(
        [w[...].reshape(w.shape[0] * w.shape[1], width) for w in words], axis=0
    )
    for i in range(count):
        tall = jnp.concatenate(
            [scaled(weights[k], coef.at[k], start + i, per) for k in range(total)], axis=0
        )
        result[i] = lax.dot_general(tall, word_rows, TN, preferred_element_type=F32).astype(BF16)
        save(i).start()
    for i in range(count):
        save(i).wait()


def patch_call(coef, weights, words, shape, start, count, prior=()):
    total = len(weights)
    flat = [piece for pieces in words for piece in pieces]
    args = (*near(coef, *weights, *flat), *prior)
    return pl.pallas_call(
        functools.partial(patch_kernel, total, start, tuple(len(p) for p in words)),
        out_shape=jax.ShapeDtypeStruct(shape, BF16),
        in_specs=[spec()] * (1 + total + len(flat)) + [spec(pl.ANY)] * len(prior),
        out_specs=spec(pl.ANY),
        scratch_shapes=[
            pltpu.VMEM((count, *shape[1:]), BF16),
            pltpu.SemaphoreType.DMA((count,)),
        ],
        input_output_aliases={len(args) - 1: 0} if prior else {},
        compiler_params=params(16),
        cost_estimate=tiny(),
        name=f"patch_{start}",
    )(*args)


def half_kernel(start, x, out):
    out[...] = x[start : start + out.shape[0]]


def half_call(start, x):
    count = x.shape[0] // 2
    return pl.pallas_call(
        functools.partial(half_kernel, start),
        out_shape=pltpu.VMEM((count, *x.shape[1:]), x.dtype),
        in_specs=[spec()],
        out_specs=spec(),
        compiler_params=params(4),
        cost_estimate=tiny(),
        name=f"half_{start}",
    )(*near(x))


def join_kernel(low, high, sibling, low_out, high_out):
    half = low.shape[0]
    low_out[...] = (low[...] + sibling[:half].astype(F32)).astype(low_out.dtype)
    high_out[...] = (high[...] + sibling[half:].astype(F32)).astype(high_out.dtype)


def join_call(name, low, high, sibling, low_type, high_type):
    return pl.pallas_call(
        join_kernel,
        out_shape=(pltpu.VMEM(low.shape, low_type), pltpu.VMEM(high.shape, high_type)),
        in_specs=[spec()] * 3,
        out_specs=(spec(),) * 2,
        compiler_params=params(4),
        cost_estimate=tiny(),
        name=name,
    )(*near(low, high, sibling))


def add_kernel(*refs):
    total = refs[0][...].astype(F32)
    for ref in refs[1:-1]:
        total = total + ref[...].astype(F32)
    refs[-1][...] = total.astype(refs[-1].dtype)


def add_call(name, dtype, *arrays):
    return pl.pallas_call(
        add_kernel,
        out_shape=pltpu.VMEM(arrays[0].shape, dtype),
        in_specs=[spec()] * len(arrays),
        out_specs=spec(),
        compiler_params=params(4),
        cost_estimate=tiny(),
        name=name,
    )(*near(*arrays))


def total_kernel(lows, highs, *refs):
    out = refs[-1]
    half = out.shape[0] // 2
    wholes = refs[lows + highs : -1]
    for n, part in enumerate((refs[:lows], refs[lows : lows + highs])):
        here = slice(half * n, half * (n + 1))
        total = part[0][...].astype(F32)
        for ref in part[1:]:
            total = total + ref[...].astype(F32)
        for ref in wholes:
            total = total + ref[here].astype(F32)
        out[here] = total.astype(out.dtype)


def total_call(name, lows, highs, wholes, out):
    return pl.pallas_call(
        functools.partial(total_kernel, len(lows), len(highs)),
        out_shape=out,
        in_specs=[spec()] * (len(lows) + len(highs) + len(wholes)),
        out_specs=spec(),
        compiler_params=params(8),
        cost_estimate=tiny(),
        name=name,
    )(*near(*lows, *highs, *wholes))


def scalar_kernel(mine, other, loss_out, temp_out):
    total = mine[...] + other[...]
    loss_out[0] = total[0, 0]
    temp_out[0] = total[1, 0]


def scalar_call(mine, other):
    one = jax.ShapeDtypeStruct((1,), F32)
    return pl.pallas_call(
        scalar_kernel,
        out_shape=(one, one),
        in_specs=[spec()] * 2,
        out_specs=(spec(pltpu.SMEM), spec(pltpu.SMEM)),
        compiler_params=params(4),
        cost_estimate=tiny(),
        name="scalars",
    )(*near(mine, other))


def body(patches, words, natural_sharpness_exponent, candidates, counts):
    total = lax.axis_size("cap")
    rows = lax.axis_size("img")
    per, patch, width = patches.shape
    images = per * total * rows
    groups = total // 2
    half = per // 2
    bits = [1 << n for n in range(groups.bit_length() - 1)]
    barrier = lax.optimization_barrier

    def low_bit(g):
        return g & -g

    def high_bit(g):
        return 1 << (g.bit_length() - 1)

    def hop(x, offset):
        return lax.ppermute(x, "cap", [(i, i ^ offset) for i in range(total)])

    words_at = [None] * total
    words_at[0] = (words,)
    for b in bits:
        words_at[2 * b] = (hop(words, 2 * b),)
    words_at[1] = (hop(words, 1),)

    meta = None
    weights, scores, products = [], [], {}

    def forward(k):
        nonlocal meta
        if k:
            extra = (meta, scores[-1])
        else:
            extra = (jnp.transpose(candidates, (2, 0, 1)), counts, natural_sharpness_exponent)
        product = k < 2 or k // 2 in bits
        made = forward_call(k, total, product, patches, words_at[k], extra)
        if not k:
            meta = made[-1]
        weights.append(made[0])
        scores.append(made[1])
        if product:
            products[k] = made[2]

    forward(0)
    forward(1)
    for b in bits:
        words_at[2 * b] = barrier((words_at[2 * b][0], scores[-1]))[:1]

    def part(g, side):
        pieces = words_at[2 * g]
        return pieces[side] if len(pieces) == 2 else half_call(side * half, pieces[0])

    for g in range(1, groups):
        if words_at[2 * g] is None:
            words_at[2 * g] = (
                hop(part(g ^ high_bit(g), 0), 2 * high_bit(g)),
                hop(part(g ^ low_bit(g), 1), 2 * low_bit(g)),
            )
    for b in bits:
        words_at[2 * b + 1] = (hop(words_at[2 * b][0], 1),)
    sequence = bits + [g for g in range(1, groups) if g not in bits]
    order = [0, 1] + [2 * g + n for g in sequence for n in (0, 1)]
    done = 2
    for g in sequence:
        if words_at[2 * g + 1] is None:
            *pieces, _ = barrier((*words_at[2 * g], scores[-1]))
            words_at[2 * g] = tuple(pieces)
            words_at[2 * g + 1] = tuple(hop(x, 1) for x in pieces)
        forward(2 * g)
        forward(2 * g + 1)
    by_offset = dict(zip(order, weights))
    weights = [by_offset[k] for k in range(total)]
    scores = scores[-1]

    pair = pair_call(per, scores, hop(scores, 1))
    tiles = [pair] + [hop(pair, 2 * g) for g in range(1, groups)]
    coef, sums = stats_call(images, per, width, meta, tiles)

    lows = [[] for _ in range(groups)]
    highs = [[] for _ in range(groups)]
    wholes = [[] for _ in range(groups)]
    mixed = []

    def word(g, coef):
        if 2 * g in products:
            sources = (products[2 * g], products[2 * g + 1])
        else:
            sources = (weights[2 * g], weights[2 * g + 1], (patches,))
        low, high, theirs = word_call(g, total, words.shape, meta, coef, *sources)
        lows[g].append(low)
        highs[g].append(high)
        wholes[g].append(hop(theirs, 1))

    far = [g for g in range(1, groups) if g not in bits]
    for g in sorted(far, key=lambda g: -bin(g).count("1")) + bits:
        word(g, coef)
    for g in far:
        low, high = join_call(
            f"join_{g}",
            lows[g].pop(),
            highs[g].pop(),
            wholes[g].pop(),
            BF16 if g & 1 else F32,
            BF16 if g & bits[-1] else F32,
        )
        lows[g].append(low)
        highs[g].append(high)
    near_coef = barrier((coef, *(lows[far[-1]] if far else [])))[0]
    word(0, near_coef)

    step = 1
    while 2 * step < rows:
        other = lax.ppermute(sums, "img", [(i, i ^ step) for i in range(rows)])
        sums = add_call(f"sums_{step}", F32, sums, other)
        step *= 2

    def pass_on(store, g, b, name):
        terms = store[g]
        value = terms[0] if len(terms) == 1 else add_call(name, BF16, *terms)
        store[g ^ b].append(hop(value, 2 * b))

    for b in bits:
        for g in reversed(far):
            if low_bit(g) == b:
                pass_on(lows, g, b, f"low_{g}")
    for b in reversed(bits):
        for g in reversed(far):
            if high_bit(g) == b:
                pass_on(highs, g, b, f"high_{g}")
    block = pltpu.VMEM(words.shape, BF16)
    for b in reversed(bits):
        first, *rest = lows[b]
        first, _ = barrier((first, sums))
        value = total_call(f"mix_{b}", [first, *rest], highs[b], wholes[b], block)
        mixed.append(value)
        wholes[0].append(hop(value, 2 * b))

    late_coef, *_ = barrier((coef, *mixed))
    patch_grad = patch_call(late_coef, weights, words_at, patches.shape, 0, per // 2)
    sums, patch_grad = barrier((sums, patch_grad))
    other = lax.ppermute(sums, "img", [(i, i ^ step) for i in range(rows)])
    patch_grad = patch_call(
        late_coef, weights, words_at, patches.shape, per // 2, per - per // 2, (patch_grad,)
    )
    word_grad = total_call(
        "finish", lows[0], highs[0], wholes[0], jax.ShapeDtypeStruct(words.shape, BF16)
    )
    other, word_grad = barrier((other, word_grad))
    loss, temp = scalar_call(sums, other)
    return patch_grad, word_grad, loss, temp


def solution(mesh):
    placed = (P(("img", "cap"), None, None), P(("img", "cap"), None, None), P(), P(), P())
    return jax.shard_map(
        body,
        mesh=mesh,
        in_specs=placed,
        out_specs=(P(("img", "cap"), None, None), P(("img", "cap"), None, None), P(), P()),
        check_vma=False,
    )
```

```python
import functools
import math

import jax
import jax.numpy as jnp
from jax import lax
from jax.experimental import pallas as pl
from jax.experimental.pallas import tpu as pltpu
from jax.sharding import PartitionSpec as P

sharpness = 4.0
loss_scale = 65536.0
far_below = -1e30
F32 = jnp.float32
BF16 = jnp.bfloat16
LANES = 128
ROWS = 8

NT = (((1,), (1,)), ((), ()))
NN = (((1,), (0,)), ((), ()))
TN = (((0,), (0,)), ((), ()))


def spec(space=pltpu.VMEM):
    return pl.BlockSpec(memory_space=space)


def near(*arrays):
    return tuple(pltpu.with_memory_space_constraint(x, pltpu.VMEM) for x in arrays)


def tiny():
    return pl.CostEstimate(flops=1, bytes_accessed=1, transcendentals=0)


def params(mib):
    return pltpu.CompilerParams(vmem_limit_bytes=mib << 20)


def fill_meta(cands, counts, nse, per, total, meta):
    row = lax.axis_index("img")
    me = lax.axis_index("cap")
    slots = cands.shape[0]
    sub = lax.broadcasted_iota(jnp.int32, (ROWS, LANES), 0)
    lane = lax.broadcasted_iota(jnp.int32, (ROWS, LANES), 1)
    column = lane // per
    first = sub < per
    for g in range(total // 2):
        even, odd = me ^ (2 * g), me ^ (2 * g + 1)
        live = jnp.zeros((ROWS, LANES), F32)
        for s in range(slots):
            here = jnp.where(s < counts[row, even], cands[s, row, even], -1)
            there = jnp.where(s < counts[row, odd], cands[s, row, odd], -1)
            live = jnp.where(column == jnp.where(first, here, there), 1.0, live)
        meta[g] = jnp.where(sub < 2 * per, live, 0.0)
    for part in range(total // ROWS):
        live = jnp.zeros((ROWS, LANES), F32)
        for s in range(slots):
            target = jnp.where(s < counts[row, me], cands[s, row, me], -1)
            live = jnp.where((me ^ (sub + ROWS * part)) == target, 1.0, live)
        meta[total // 2 + part] = live
    meta[meta.shape[0] - 1] = jnp.exp(jnp.full((ROWS, LANES), nse[0], F32))


def block_is_live(meta, total, offset):
    return meta[total // 2 + offset // ROWS, offset % ROWS, 0] > 0.0


def forward_kernel(offset, pieces, total, product, *refs):
    fetched = ()
    if offset:
        meta, patches, prior, *words = refs[: 3 + pieces]
        outs = refs[3 + pieces :]
    else:
        cands_far, counts_far, nse, patches_far, words_far = refs[:5]
        *outs, patches, near_words, cands, counts, sems = refs[5:]
        words = [near_words]
        moves = [(cands_far, cands), (counts_far, counts), (words_far, near_words)]
        moves += [(patches_far.at[i], patches.at[i]) for i in range(patches.shape[0])]
        copies = [pltpu.make_async_copy(a, b, sems.at[n]) for n, (a, b) in enumerate(moves)]
        for copy in copies[2:]:
            copy.start()
        for copy in copies[:2]:
            copy.start()
        fetched = copies[3:]
    weights_out, scores_out = outs[:2]
    me = lax.axis_index("cap")
    column = me ^ offset
    per, patch, width = patches.shape
    tokens = words[0].shape[1]
    lines = per * tokens
    scale = sharpness * width**-0.5 * math.log2(math.e)

    def start():
        scores_out[...] = prior[...] if offset else jnp.zeros(scores_out.shape, F32)

    start()
    if not offset:
        copies[2].wait()

    def score():
        sub = lax.broadcasted_iota(jnp.int32, (ROWS, LANES), 0)
        lane = lax.broadcasted_iota(jnp.int32, (ROWS, LANES), 1)
        spot = lane == column * per + sub

        def place(i, over_words, over_patches):
            part = jnp.sum(over_words, axis=1, keepdims=True) * (1.0 / patch)
            part = part + over_patches * (1.0 / tokens)
            part = part * (0.5 * math.log(2.0) / sharpness)
            part = jnp.concatenate([part, jnp.zeros((ROWS - per, 1), F32)], axis=0)
            line = jnp.sum(jnp.where(spot & (sub < per), part, 0.0), axis=0, keepdims=True)
            return jnp.where(sub == i, line, 0.0)

        word_rows = jnp.concatenate(
            [w[...].reshape(w.shape[0] * tokens, width) for w in words], axis=0
        )
        low = high = None
        tile = jnp.zeros((ROWS, LANES), F32)
        for i in range(per):
            if fetched:
                fetched[i].wait()
            raw = lax.dot_general(word_rows, patches[i], NT, preferred_element_type=F32)
            mass = jnp.exp2(raw * scale)
            mass3 = mass.reshape(per, tokens, patch)
            word_sum = jnp.sum(mass3, axis=1)
            patch_sum = jnp.sum(mass, axis=1, keepdims=True)
            least = jnp.minimum(
                jnp.min(word_sum, axis=0, keepdims=True),
                jnp.min(patch_sum, axis=0, keepdims=True),
            )
            most = jnp.maximum(
                jnp.max(word_sum, axis=0, keepdims=True),
                jnp.max(patch_sum, axis=0, keepdims=True),
            )
            low = least if low is None else jnp.minimum(low, least)
            high = most if high is None else jnp.maximum(high, most)
            word_part = (0.5 / patch) / word_sum
            patch_part = (0.5 / tokens) / patch_sum
            blended = mass3 * (word_part[:, None, :] + patch_part.reshape(per, tokens, 1))
            weights_out[i] = blended.reshape(lines, patch).astype(BF16)
            patch_logs = jnp.sum(jnp.log2(patch_sum).reshape(per, tokens, 1), axis=1)
            tile = tile + place(i, jnp.log2(word_sum), patch_logs)
        scores_out[...] += tile
        safe = (jnp.min(low) > 2.0**-90) & (jnp.max(high) < 2.0**120)

        @pl.when(jnp.logical_not(safe))
        def _():
            start()

            def image(i, carry):
                raw = lax.dot_general(word_rows, patches[i], NT, preferred_element_type=F32)
                lifted = raw * scale
                lifted3 = lifted.reshape(per, tokens, patch)
                word_top = jnp.max(lifted3, axis=1)
                patch_top = jnp.max(lifted, axis=1, keepdims=True)
                word_mass = jnp.exp2(lifted3 - word_top[:, None, :])
                patch_mass = jnp.exp2(lifted - patch_top).reshape(per, tokens, patch)
                word_sum = jnp.sum(word_mass, axis=1)
                patch_sum = jnp.sum(patch_mass, axis=2, keepdims=True)
                word_part = (0.5 / patch) / word_sum
                patch_part = (0.5 / tokens) / patch_sum
                blended = word_mass * word_part[:, None, :] + patch_mass * patch_part
                weights_out[i] = blended.reshape(lines, patch).astype(BF16)
                patch_logs = jnp.sum(
                    patch_top.reshape(per, tokens, 1) + jnp.log2(patch_sum), axis=1
                )
                scores_out[...] += place(i, word_top + jnp.log2(word_sum), patch_logs)
                return carry

            lax.fori_loop(0, per, image, 0)

        if product:
            for i in range(per):
                outs[2][i] = lax.dot_general(
                    weights_out[i], patches[i], NN, preferred_element_type=F32
                )

    if offset:
        live = block_is_live(meta, total, offset)
        pl.when(live)(score)

        @pl.when(jnp.logical_not(live))
        def _():
            weights_out[...] = jnp.zeros(weights_out.shape, weights_out.dtype)

    else:
        score()
        for copy in copies[:2]:
            copy.wait()
        fill_meta(cands, counts, nse, per, total, outs[-1])


def forward_call(offset, total, product, patches, words, extra):
    per, patch, width = patches.shape
    lines = per * words[0].shape[1]
    shapes = (pltpu.VMEM((per, lines, patch), BF16), pltpu.VMEM((ROWS, LANES), F32))
    scratch = []
    if product:
        shapes += (pltpu.VMEM((per, lines, width), F32),)
    if offset:
        meta, prior = extra
        args = near(meta, patches, prior, *words)
        specs = [spec()] * len(args)
    else:
        cands, counts, nse = extra
        args = [cands, counts, patches, *words]
        args = [pltpu.with_memory_space_constraint(x, pltpu.HBM) for x in args]
        args.insert(2, nse)
        specs = [spec(pl.ANY)] * 2 + [spec(pltpu.SMEM)] + [spec(pl.ANY)] * 2
        shapes += (
            pltpu.VMEM((total // 2 + total // ROWS + 1, ROWS, LANES), F32),
            pltpu.VMEM(patches.shape, BF16),
            pltpu.VMEM(words[0].shape, BF16),
        )
        scratch = [
            pltpu.SMEM(cands.shape, jnp.int32),
            pltpu.SMEM(counts.shape, jnp.int32),
            pltpu.SemaphoreType.DMA((3 + per,)),
        ]
    return pl.pallas_call(
        functools.partial(forward_kernel, offset, len(words), total, product),
        out_shape=shapes,
        in_specs=specs,
        out_specs=(spec(),) * len(shapes),
        scratch_shapes=scratch,
        compiler_params=params(12),
        cost_estimate=tiny(),
        name=f"forward_{offset}",
    )(*args)


def stats_kernel(total, images, per, width, meta, *refs):
    tiles = refs[: total // 2]
    coef_out, sums_out = refs[total // 2 :]
    me = lax.axis_index("cap")
    sub = lax.broadcasted_iota(jnp.int32, (ROWS, LANES), 0)
    lane = lax.broadcasted_iota(jnp.int32, (ROWS, LANES), 1)
    first = sub < per
    image = jnp.where(first, sub, sub - per)
    softness = meta[meta.shape[0] - 1]
    kept, lives, marks = [], [], []
    peak = jnp.full((1, LANES), far_below, F32)
    for g in range(total // 2):
        even, odd = me ^ (2 * g), me ^ (2 * g + 1)
        live = meta[g] > 0.0
        masked = jnp.where(live, tiles[g][...] * softness, far_below)
        kept.append(masked)
        lives.append(live)
        marks.append(live & (lane == jnp.where(first, even, odd) * per + image))
        peak = jnp.maximum(peak, jnp.max(masked, axis=0, keepdims=True))
    mass = jnp.zeros((1, LANES), F32)
    for masked, live in zip(kept, lives):
        mass = mass + jnp.sum(
            jnp.where(live, jnp.exp(masked - peak), 0.0), axis=0, keepdims=True
        )
    col_ok = lane[:1] < total * per
    col_lse = jnp.where(col_ok, peak + jnp.log(jnp.where(col_ok, mass, 1.0)), 0.0)
    loss = jnp.where(sub == 0, col_lse, 0.0)
    temp = jnp.zeros((ROWS, LANES), F32)
    pulls = []
    for masked, live, mark in zip(kept, lives, marks):
        top = jnp.max(masked, axis=1, keepdims=True)
        part = jnp.sum(jnp.where(live, jnp.exp(masked - top), 0.0), axis=1, keepdims=True)
        row_lse = top + jnp.log(jnp.where(sub[:, :1] < 2 * per, part, 1.0))
        pull = jnp.where(
            live,
            (0.5 / images)
            * (jnp.exp(masked - row_lse) + jnp.exp(masked - col_lse) - jnp.where(mark, 2.0, 0.0)),
            0.0,
        )
        pulls.append(pull)
        temp = temp + jnp.where(live, pull * masked, 0.0)
        loss = loss + jnp.where((lane == 0) & (sub < 2 * per), row_lse, 0.0)
        loss = loss - jnp.where(mark, 2.0 * masked, 0.0)
    loss_total = jnp.sum(loss) * (0.5 / images)
    temp_total = jnp.sum(temp)
    sums_out[...] = jnp.where(sub == 0, loss_total, temp_total)
    factor = pulls[0] * softness * (loss_scale * width**-0.5)
    for k in range(total):
        spot = (lane == (me ^ k) * per + sub) & first
        for i in range(per):
            line = jnp.broadcast_to(factor[i : i + 1], (ROWS, LANES))
            value = jnp.sum(jnp.where(spot, line, 0.0), axis=1, keepdims=True)
            coef_out[k, i] = jnp.broadcast_to(value, (ROWS, LANES))


def stats_call(images, per, width, meta, tiles):
    total = 2 * len(tiles)
    return pl.pallas_call(
        functools.partial(stats_kernel, total, images, per, width),
        out_shape=(
            pltpu.VMEM((total, per, ROWS, LANES), F32),
            pltpu.VMEM((ROWS, LANES), F32),
        ),
        in_specs=[spec()] * (1 + len(tiles)),
        out_specs=(spec(), spec()),
        compiler_params=params(4),
        cost_estimate=tiny(),
        name="stats",
    )(*near(meta, *tiles))


def pair_kernel(per, own, other, out):
    sub = lax.broadcasted_iota(jnp.int32, (ROWS, LANES), 0)
    moved = jnp.concatenate([other[...]] * 2, axis=0)[ROWS - per : 2 * ROWS - per]
    out[...] = jnp.where(sub < per, own[...], moved)


def pair_call(per, own, other):
    return pl.pallas_call(
        functools.partial(pair_kernel, per),
        out_shape=pltpu.VMEM((ROWS, LANES), F32),
        in_specs=[spec()] * 2,
        out_specs=spec(),
        compiler_params=params(4),
        cost_estimate=tiny(),
        name="pair",
    )(*near(own, other))


def scaled(weights, coef, i, per):
    lines, patch = weights.shape[1:]
    block = weights[i].astype(F32).reshape(per, lines // per, patch)
    factor = jnp.tile(coef[i, :per][:, None, :], (1, 1, patch // LANES))
    return (block * factor).reshape(lines, patch).astype(BF16)


def word_kernel(group, total, patches, meta, coef, source_a, source_b, low_out, high_out, out_b):
    half, tokens, width = low_out.shape
    per = 2 * half
    for n, source in enumerate((source_a, source_b)):
        offset = 2 * group + n
        shape = (per, tokens, width)

        def put(value):
            if n:
                out_b[...] = value.astype(out_b.dtype)
            else:
                low_out[...] = value[:half]
                high_out[...] = value[half:]

        def run():
            if patches is None:
                value = jnp.zeros(shape, F32)
                for i in range(per):
                    factor = jnp.tile(coef[offset, i, :per][:, None, :], (1, 1, width // LANES))
                    value = value + source[i].reshape(shape) * factor
                put(value)
                return
            wide = jnp.concatenate(
                [scaled(source, coef.at[offset], i, per) for i in range(per)], axis=1
            )
            rows = patches[...].reshape(-1, width)
            put(lax.dot_general(wide, rows, NN, preferred_element_type=F32).reshape(shape))

        if offset:
            live = block_is_live(meta, total, offset)
            pl.when(live)(run)
            pl.when(jnp.logical_not(live))(lambda: put(jnp.zeros(shape, F32)))
        else:
            run()


def word_products(group, total, meta, coef, *refs):
    word_kernel(group, total, None, meta, coef, *refs)


def word_blends(group, total, patches, meta, coef, *refs):
    word_kernel(group, total, patches, meta, coef, *refs)


def word_call(group, total, shape, meta, coef, source_a, source_b, patches=()):
    part = (shape[0] // 2, *shape[1:])
    return pl.pallas_call(
        functools.partial(word_blends if patches else word_products, group, total),
        out_shape=(pltpu.VMEM(part, F32), pltpu.VMEM(part, F32), pltpu.VMEM(shape, BF16)),
        in_specs=[spec()] * (4 + len(patches)),
        out_specs=(spec(),) * 3,
        compiler_params=params(12),
        cost_estimate=tiny(),
        name=f"word_{group}",
    )(*near(*patches, meta, coef, source_a, source_b))


def patch_kernel(total, start, split, coef, *refs):
    out, result, sems = refs[-3:]
    weights, words = refs[:total], refs[total : total + sum(split)]
    count, patch, width = result.shape
    per = out.shape[0]

    def save(i):
        return pltpu.make_async_copy(result.at[i], out.at[start + i], sems.at[i])

    word_rows = jnp.concatenate(
        [w[...].reshape(w.shape[0] * w.shape[1], width) for w in words], axis=0
    )
    for i in range(count):
        tall = jnp.concatenate(
            [scaled(weights[k], coef.at[k], start + i, per) for k in range(total)], axis=0
        )
        result[i] = lax.dot_general(tall, word_rows, TN, preferred_element_type=F32).astype(BF16)
        save(i).start()
    for i in range(count):
        save(i).wait()


def patch_call(coef, weights, words, shape, start, count, prior=()):
    total = len(weights)
    flat = [piece for pieces in words for piece in pieces]
    args = (*near(coef, *weights, *flat), *prior)
    return pl.pallas_call(
        functools.partial(patch_kernel, total, start, tuple(len(p) for p in words)),
        out_shape=jax.ShapeDtypeStruct(shape, BF16),
        in_specs=[spec()] * (1 + total + len(flat)) + [spec(pl.ANY)] * len(prior),
        out_specs=spec(pl.ANY),
        scratch_shapes=[
            pltpu.VMEM((count, *shape[1:]), BF16),
            pltpu.SemaphoreType.DMA((count,)),
        ],
        input_output_aliases={len(args) - 1: 0} if prior else {},
        compiler_params=params(16),
        cost_estimate=tiny(),
        name=f"patch_{start}",
    )(*args)


def half_kernel(start, x, out):
    out[...] = x[start : start + out.shape[0]]


def half_call(start, x):
    count = x.shape[0] // 2
    return pl.pallas_call(
        functools.partial(half_kernel, start),
        out_shape=pltpu.VMEM((count, *x.shape[1:]), x.dtype),
        in_specs=[spec()],
        out_specs=spec(),
        compiler_params=params(4),
        cost_estimate=tiny(),
        name=f"half_{start}",
    )(*near(x))


def join_kernel(low, high, sibling, low_out, high_out):
    half = low.shape[0]
    low_out[...] = (low[...] + sibling[:half].astype(F32)).astype(low_out.dtype)
    high_out[...] = (high[...] + sibling[half:].astype(F32)).astype(high_out.dtype)


def join_call(name, low, high, sibling, low_type, high_type):
    return pl.pallas_call(
        join_kernel,
        out_shape=(pltpu.VMEM(low.shape, low_type), pltpu.VMEM(high.shape, high_type)),
        in_specs=[spec()] * 3,
        out_specs=(spec(),) * 2,
        compiler_params=params(4),
        cost_estimate=tiny(),
        name=name,
    )(*near(low, high, sibling))


def add_kernel(*refs):
    total = refs[0][...].astype(F32)
    for ref in refs[1:-1]:
        total = total + ref[...].astype(F32)
    refs[-1][...] = total.astype(refs[-1].dtype)


def add_call(name, dtype, *arrays):
    return pl.pallas_call(
        add_kernel,
        out_shape=pltpu.VMEM(arrays[0].shape, dtype),
        in_specs=[spec()] * len(arrays),
        out_specs=spec(),
        compiler_params=params(4),
        cost_estimate=tiny(),
        name=name,
    )(*near(*arrays))


def total_kernel(lows, highs, *refs):
    out = refs[-1]
    half = out.shape[0] // 2
    wholes = refs[lows + highs : -1]
    for n, part in enumerate((refs[:lows], refs[lows : lows + highs])):
        here = slice(half * n, half * (n + 1))
        total = part[0][...].astype(F32)
        for ref in part[1:]:
            total = total + ref[...].astype(F32)
        for ref in wholes:
            total = total + ref[here].astype(F32)
        out[here] = total.astype(out.dtype)


def total_call(name, lows, highs, wholes, out):
    return pl.pallas_call(
        functools.partial(total_kernel, len(lows), len(highs)),
        out_shape=out,
        in_specs=[spec()] * (len(lows) + len(highs) + len(wholes)),
        out_specs=spec(),
        compiler_params=params(8),
        cost_estimate=tiny(),
        name=name,
    )(*near(*lows, *highs, *wholes))


def finish_kernel(lows, highs, mine, other, *refs):
    word_out, loss_out, temp_out = refs[-3:]
    total_kernel(lows, highs, *refs[:-2])
    total = mine[...] + other[...]
    loss_out[0] = total[0, 0]
    temp_out[0] = total[1, 0]


def finish_call(mine, other, lows, highs, wholes, shape):
    one = jax.ShapeDtypeStruct((1,), F32)
    return pl.pallas_call(
        functools.partial(finish_kernel, len(lows), len(highs)),
        out_shape=(jax.ShapeDtypeStruct(shape, BF16), one, one),
        in_specs=[spec()] * (2 + len(lows) + len(highs) + len(wholes)),
        out_specs=(spec(), spec(pltpu.SMEM), spec(pltpu.SMEM)),
        compiler_params=params(8),
        cost_estimate=tiny(),
        name="finish",
    )(*near(mine, other, *lows, *highs, *wholes))


def body(patches, words, natural_sharpness_exponent, candidates, counts):
    total = lax.axis_size("cap")
    rows = lax.axis_size("img")
    per, patch, width = patches.shape
    images = per * total * rows
    groups = total // 2
    half = per // 2
    bits = [1 << n for n in range(groups.bit_length() - 1)]
    barrier = lax.optimization_barrier

    def low_bit(g):
        return g & -g

    def high_bit(g):
        return 1 << (g.bit_length() - 1)

    def hop(x, offset):
        return lax.ppermute(x, "cap", [(i, i ^ offset) for i in range(total)])

    words_at = [None] * total
    words_at[0] = (words,)
    for b in bits:
        words_at[2 * b] = (hop(words, 2 * b),)
    words_at[1] = (hop(words, 1),)

    meta = None
    weights, scores, products = [], [], {}

    def forward(k):
        nonlocal meta, patches
        if k:
            extra = (meta, scores[-1])
        else:
            extra = (jnp.transpose(candidates, (2, 0, 1)), counts, natural_sharpness_exponent)
        product = k < 2 or k // 2 in bits
        made = forward_call(k, total, product, patches, words_at[k], extra)
        if not k:
            meta, patches, near_words = made[-3:]
            words_at[0] = (near_words,)
        weights.append(made[0])
        scores.append(made[1])
        if product:
            products[k] = made[2]

    forward(0)
    forward(1)
    for b in bits:
        words_at[2 * b] = barrier((words_at[2 * b][0], scores[-1]))[:1]

    def part(g, side):
        pieces = words_at[2 * g]
        return pieces[side] if len(pieces) == 2 else half_call(side * half, pieces[0])

    for g in range(1, groups):
        if words_at[2 * g] is None:
            words_at[2 * g] = (
                hop(part(g ^ high_bit(g), 0), 2 * high_bit(g)),
                hop(part(g ^ low_bit(g), 1), 2 * low_bit(g)),
            )
    for b in bits:
        words_at[2 * b + 1] = (hop(words_at[2 * b][0], 1),)
    sequence = bits + [g for g in range(1, groups) if g not in bits]
    order = [0, 1] + [2 * g + n for g in sequence for n in (0, 1)]
    done = 2
    for g in sequence:
        if words_at[2 * g + 1] is None:
            *pieces, _ = barrier((*words_at[2 * g], scores[-1]))
            words_at[2 * g] = tuple(pieces)
            words_at[2 * g + 1] = tuple(hop(x, 1) for x in pieces)
        forward(2 * g)
        forward(2 * g + 1)
    by_offset = dict(zip(order, weights))
    weights = [by_offset[k] for k in range(total)]
    scores = scores[-1]

    pair = pair_call(per, scores, hop(scores, 1))
    tiles = [pair] + [hop(pair, 2 * g) for g in range(1, groups)]
    coef, sums = stats_call(images, per, width, meta, tiles)

    lows = [[] for _ in range(groups)]
    highs = [[] for _ in range(groups)]
    wholes = [[] for _ in range(groups)]
    mixed = []

    def word(g, coef):
        if 2 * g in products:
            sources = (products[2 * g], products[2 * g + 1])
        else:
            sources = (weights[2 * g], weights[2 * g + 1], (patches,))
        low, high, theirs = word_call(g, total, words.shape, meta, coef, *sources)
        lows[g].append(low)
        highs[g].append(high)
        wholes[g].append(hop(theirs, 1))

    far = [g for g in range(1, groups) if g not in bits]
    for g in sorted(far, key=lambda g: -bin(g).count("1")) + bits:
        word(g, coef)
    for g in far + bits:
        low, high = join_call(
            f"join_{g}",
            lows[g].pop(),
            highs[g].pop(),
            wholes[g].pop(),
            BF16 if g & 1 else F32,
            BF16 if g & bits[-1] else F32,
        )
        lows[g].append(low)
        highs[g].append(high)
    word(0, barrier((coef, *(lows[b][0] for b in bits), *(highs[b][0] for b in bits)))[0])

    step = 1
    while 2 * step < rows:
        other = lax.ppermute(sums, "img", [(i, i ^ step) for i in range(rows)])
        sums = add_call(f"sums_{step}", F32, sums, other)
        step *= 2

    early = []

    def pass_on(store, g, b, name):
        terms = store[g]
        value = terms[0]
        if len(terms) > 1:
            *terms, _ = barrier((*terms, sums))
            value = add_call(name, BF16, *terms)
            mixed.append(value)
        moved = hop(value, 2 * b)
        if len(terms) == 1 and g == b:
            early.append(moved)
        store[g ^ b].append(moved)

    for b in bits:
        for g in range(groups - 1, 0, -1):
            if low_bit(g) == b:
                pass_on(lows, g, b, f"low_{g}")
    for b in reversed(bits):
        for g in range(groups - 1, 0, -1):
            if high_bit(g) == b:
                pass_on(highs, g, b, f"high_{g}")

    late_coef, *_ = barrier((coef, *mixed))
    patch_grad = patch_call(late_coef, weights, words_at, patches.shape, 0, per // 2)
    sums, patch_grad = barrier((sums, patch_grad))
    other = lax.ppermute(sums, "img", [(i, i ^ step) for i in range(rows)])
    late_coef, *_ = barrier((late_coef, *early))
    patch_grad = patch_call(
        late_coef, weights, words_at, patches.shape, per // 2, per - per // 2, (patch_grad,)
    )
    word_grad, loss, temp = finish_call(
        sums, other, lows[0], highs[0], wholes[0], words.shape
    )
    return patch_grad, word_grad, loss, temp


def solution(mesh):
    placed = (P(("img", "cap"), None, None), P(("img", "cap"), None, None), P(), P(), P())
    return jax.shard_map(
        body,
        mesh=mesh,
        in_specs=placed,
        out_specs=(P(("img", "cap"), None, None), P(("img", "cap"), None, None), P(), P()),
        check_vma=False,
    )
```

```python
import functools
import math

import jax
import jax.numpy as jnp
from jax import lax
from jax.experimental import pallas as pl
from jax.experimental.pallas import tpu as pltpu
from jax.sharding import PartitionSpec as P

sharpness = 4.0
loss_scale = 65536.0
far_below = -1e30
F32 = jnp.float32
BF16 = jnp.bfloat16
LANES = 128
ROWS = 8

NN = (((1,), (0,)), ((), ()))
TN = (((0,), (0,)), ((), ()))


def spec(space=pltpu.VMEM):
    return pl.BlockSpec(memory_space=space)


def near(*arrays):
    return tuple(pltpu.with_memory_space_constraint(x, pltpu.VMEM) for x in arrays)


def tiny():
    return pl.CostEstimate(flops=1, bytes_accessed=1, transcendentals=0)


def params(mib):
    return pltpu.CompilerParams(vmem_limit_bytes=mib << 20)


def fill_meta(cands, counts, nse, per, total, meta):
    row = lax.axis_index("img")
    me = lax.axis_index("cap")
    slots = cands.shape[0]
    sub = lax.broadcasted_iota(jnp.int32, (ROWS, LANES), 0)
    lane = lax.broadcasted_iota(jnp.int32, (ROWS, LANES), 1)
    column = lane // per
    first = sub < per
    for g in range(total // 2):
        even, odd = me ^ (2 * g), me ^ (2 * g + 1)
        live = jnp.zeros((ROWS, LANES), F32)
        for s in range(slots):
            here = jnp.where(s < counts[row, even], cands[s, row, even], -1)
            there = jnp.where(s < counts[row, odd], cands[s, row, odd], -1)
            live = jnp.where(column == jnp.where(first, here, there), 1.0, live)
        meta[g] = jnp.where(sub < 2 * per, live, 0.0)
    for part in range(total // ROWS):
        live = jnp.zeros((ROWS, LANES), F32)
        for s in range(slots):
            target = jnp.where(s < counts[row, me], cands[s, row, me], -1)
            live = jnp.where((me ^ (sub + ROWS * part)) == target, 1.0, live)
        meta[total // 2 + part] = live
    meta[meta.shape[0] - 1] = jnp.exp(jnp.full((ROWS, LANES), nse[0], F32))


def block_is_live(meta, total, offset):
    return meta[total // 2 + offset // ROWS, offset % ROWS, 0] > 0.0


def forward_kernel(offset, pieces, total, product, *refs):
    fetched = ()
    if offset:
        meta, patches, turned, prior, *words = refs[: 4 + pieces]
        outs = refs[4 + pieces :]
    else:
        cands_far, counts_far, nse, patches_far, words_far = refs[:5]
        *outs, patches, turned, near_words, cands, counts, sems = refs[5:]
        words = [near_words]
        moves = [(cands_far, cands), (counts_far, counts), (words_far, near_words)]
        moves += [(patches_far.at[i], patches.at[i]) for i in range(patches.shape[0])]
        copies = [pltpu.make_async_copy(a, b, sems.at[n]) for n, (a, b) in enumerate(moves)]
        for copy in copies[2:]:
            copy.start()
        for copy in copies[:2]:
            copy.start()
        fetched = copies[3:]
    weights_out, scores_out = outs[:2]
    me = lax.axis_index("cap")
    column = me ^ offset
    per, patch, width = patches.shape
    tokens = words[0].shape[1]
    lines = per * tokens
    scale = sharpness * width**-0.5 * math.log2(math.e)

    def start():
        scores_out[...] = prior[...] if offset else jnp.zeros(scores_out.shape, F32)

    start()
    if not offset:
        copies[2].wait()

    def score():
        sub = lax.broadcasted_iota(jnp.int32, (ROWS, LANES), 0)
        lane = lax.broadcasted_iota(jnp.int32, (ROWS, LANES), 1)
        spot = lane == column * per + sub

        def place(i, over_words, over_patches):
            part = jnp.sum(over_words, axis=1, keepdims=True) * (1.0 / patch)
            part = part + over_patches * (1.0 / tokens)
            part = part * (0.5 * math.log(2.0) / sharpness)
            part = jnp.concatenate([part, jnp.zeros((ROWS - per, 1), F32)], axis=0)
            line = jnp.sum(jnp.where(spot & (sub < per), part, 0.0), axis=0, keepdims=True)
            return jnp.where(sub == i, line, 0.0)

        word_rows = jnp.concatenate(
            [w[...].reshape(w.shape[0] * tokens, width) for w in words], axis=0
        )
        low = high = None
        tile = jnp.zeros((ROWS, LANES), F32)
        for i in range(per):
            if fetched:
                fetched[i].wait()
                turned[i] = patches[i].T
            raw = lax.dot_general(word_rows, turned[i], NN, preferred_element_type=F32)
            mass = jnp.exp2(raw * scale)
            mass3 = mass.reshape(per, tokens, patch)
            word_sum = jnp.sum(mass3, axis=1)
            patch_sum = jnp.sum(mass, axis=1, keepdims=True)
            least = jnp.minimum(
                jnp.min(word_sum, axis=0, keepdims=True),
                jnp.min(patch_sum, axis=0, keepdims=True),
            )
            most = jnp.maximum(
                jnp.max(word_sum, axis=0, keepdims=True),
                jnp.max(patch_sum, axis=0, keepdims=True),
            )
            low = least if low is None else jnp.minimum(low, least)
            high = most if high is None else jnp.maximum(high, most)
            word_part = (0.5 / patch) / word_sum
            patch_part = (0.5 / tokens) / patch_sum
            blended = mass3 * (word_part[:, None, :] + patch_part.reshape(per, tokens, 1))
            weights_out[i] = blended.reshape(lines, patch).astype(BF16)
            patch_logs = jnp.sum(jnp.log2(patch_sum).reshape(per, tokens, 1), axis=1)
            tile = tile + place(i, jnp.log2(word_sum), patch_logs)
        scores_out[...] += tile
        safe = (jnp.min(low) > 2.0**-90) & (jnp.max(high) < 2.0**120)

        @pl.when(jnp.logical_not(safe))
        def _():
            start()

            def image(i, carry):
                raw = lax.dot_general(word_rows, turned[i], NN, preferred_element_type=F32)
                lifted = raw * scale
                lifted3 = lifted.reshape(per, tokens, patch)
                word_top = jnp.max(lifted3, axis=1)
                patch_top = jnp.max(lifted, axis=1, keepdims=True)
                word_mass = jnp.exp2(lifted3 - word_top[:, None, :])
                patch_mass = jnp.exp2(lifted - patch_top).reshape(per, tokens, patch)
                word_sum = jnp.sum(word_mass, axis=1)
                patch_sum = jnp.sum(patch_mass, axis=2, keepdims=True)
                word_part = (0.5 / patch) / word_sum
                patch_part = (0.5 / tokens) / patch_sum
                blended = word_mass * word_part[:, None, :] + patch_mass * patch_part
                weights_out[i] = blended.reshape(lines, patch).astype(BF16)
                patch_logs = jnp.sum(
                    patch_top.reshape(per, tokens, 1) + jnp.log2(patch_sum), axis=1
                )
                scores_out[...] += place(i, word_top + jnp.log2(word_sum), patch_logs)
                return carry

            lax.fori_loop(0, per, image, 0)

        if product:
            for i in range(per):
                outs[2][i] = lax.dot_general(
                    weights_out[i], patches[i], NN, preferred_element_type=F32
                )

    if offset:
        live = block_is_live(meta, total, offset)
        pl.when(live)(score)

        @pl.when(jnp.logical_not(live))
        def _():
            weights_out[...] = jnp.zeros(weights_out.shape, weights_out.dtype)

    else:
        score()
        for copy in copies[:2]:
            copy.wait()
        fill_meta(cands, counts, nse, per, total, outs[-1])


def forward_call(offset, total, product, patches, turned, words, extra):
    per, patch, width = patches.shape
    lines = per * words[0].shape[1]
    shapes = (pltpu.VMEM((per, lines, patch), BF16), pltpu.VMEM((ROWS, LANES), F32))
    scratch = []
    if product:
        shapes += (pltpu.VMEM((per, lines, width), F32),)
    if offset:
        meta, prior = extra
        args = near(meta, patches, turned, prior, *words)
        specs = [spec()] * len(args)
    else:
        cands, counts, nse = extra
        args = [cands, counts, patches, *words]
        args = [pltpu.with_memory_space_constraint(x, pltpu.HBM) for x in args]
        args.insert(2, nse)
        specs = [spec(pl.ANY)] * 2 + [spec(pltpu.SMEM)] + [spec(pl.ANY)] * 2
        shapes += (
            pltpu.VMEM((total // 2 + total // ROWS + 1, ROWS, LANES), F32),
            pltpu.VMEM(patches.shape, BF16),
            pltpu.VMEM((per, width, patch), BF16),
            pltpu.VMEM(words[0].shape, BF16),
        )
        scratch = [
            pltpu.SMEM(cands.shape, jnp.int32),
            pltpu.SMEM(counts.shape, jnp.int32),
            pltpu.SemaphoreType.DMA((3 + per,)),
        ]
    return pl.pallas_call(
        functools.partial(forward_kernel, offset, len(words), total, product),
        out_shape=shapes,
        in_specs=specs,
        out_specs=(spec(),) * len(shapes),
        scratch_shapes=scratch,
        compiler_params=params(12),
        cost_estimate=tiny(),
        name=f"forward_{offset}",
    )(*args)


def stats_kernel(total, images, per, width, meta, *refs):
    tiles = refs[: total // 2]
    coef_out, sums_out = refs[total // 2 :]
    me = lax.axis_index("cap")
    sub = lax.broadcasted_iota(jnp.int32, (ROWS, LANES), 0)
    lane = lax.broadcasted_iota(jnp.int32, (ROWS, LANES), 1)
    first = sub < per
    image = jnp.where(first, sub, sub - per)
    softness = meta[meta.shape[0] - 1]
    kept, lives, marks = [], [], []
    peak = jnp.full((1, LANES), far_below, F32)
    for g in range(total // 2):
        even, odd = me ^ (2 * g), me ^ (2 * g + 1)
        live = meta[g] > 0.0
        masked = jnp.where(live, tiles[g][...] * softness, far_below)
        kept.append(masked)
        lives.append(live)
        marks.append(live & (lane == jnp.where(first, even, odd) * per + image))
        peak = jnp.maximum(peak, jnp.max(masked, axis=0, keepdims=True))
    mass = jnp.zeros((1, LANES), F32)
    for masked, live in zip(kept, lives):
        mass = mass + jnp.sum(
            jnp.where(live, jnp.exp(masked - peak), 0.0), axis=0, keepdims=True
        )
    col_ok = lane[:1] < total * per
    col_lse = jnp.where(col_ok, peak + jnp.log(jnp.where(col_ok, mass, 1.0)), 0.0)
    loss = jnp.where(sub == 0, col_lse, 0.0)
    temp = jnp.zeros((ROWS, LANES), F32)
    pulls = []
    for masked, live, mark in zip(kept, lives, marks):
        top = jnp.max(masked, axis=1, keepdims=True)
        part = jnp.sum(jnp.where(live, jnp.exp(masked - top), 0.0), axis=1, keepdims=True)
        row_lse = top + jnp.log(jnp.where(sub[:, :1] < 2 * per, part, 1.0))
        pull = jnp.where(
            live,
            (0.5 / images)
            * (jnp.exp(masked - row_lse) + jnp.exp(masked - col_lse) - jnp.where(mark, 2.0, 0.0)),
            0.0,
        )
        pulls.append(pull)
        temp = temp + jnp.where(live, pull * masked, 0.0)
        loss = loss + jnp.where((lane == 0) & (sub < 2 * per), row_lse, 0.0)
        loss = loss - jnp.where(mark, 2.0 * masked, 0.0)
    loss_total = jnp.sum(loss) * (0.5 / images)
    temp_total = jnp.sum(temp)
    sums_out[...] = jnp.where(sub == 0, loss_total, temp_total)
    factor = pulls[0] * softness * (loss_scale * width**-0.5)
    for k in range(total):
        spot = (lane == (me ^ k) * per + sub) & first
        for i in range(per):
            line = jnp.broadcast_to(factor[i : i + 1], (ROWS, LANES))
            value = jnp.sum(jnp.where(spot, line, 0.0), axis=1, keepdims=True)
            coef_out[k, i] = jnp.broadcast_to(value, (ROWS, LANES))


def stats_call(images, per, width, meta, tiles):
    total = 2 * len(tiles)
    return pl.pallas_call(
        functools.partial(stats_kernel, total, images, per, width),
        out_shape=(
            pltpu.VMEM((total, per, ROWS, LANES), F32),
            pltpu.VMEM((ROWS, LANES), F32),
        ),
        in_specs=[spec()] * (1 + len(tiles)),
        out_specs=(spec(), spec()),
        compiler_params=params(4),
        cost_estimate=tiny(),
        name="stats",
    )(*near(meta, *tiles))


def pair_kernel(per, own, other, out):
    sub = lax.broadcasted_iota(jnp.int32, (ROWS, LANES), 0)
    moved = jnp.concatenate([other[...]] * 2, axis=0)[ROWS - per : 2 * ROWS - per]
    out[...] = jnp.where(sub < per, own[...], moved)


def pair_call(per, own, other):
    return pl.pallas_call(
        functools.partial(pair_kernel, per),
        out_shape=pltpu.VMEM((ROWS, LANES), F32),
        in_specs=[spec()] * 2,
        out_specs=spec(),
        compiler_params=params(4),
        cost_estimate=tiny(),
        name="pair",
    )(*near(own, other))


def scaled(weights, coef, i, per):
    lines, patch = weights.shape[1:]
    block = weights[i].astype(F32).reshape(per, lines // per, patch)
    factor = jnp.tile(coef[i, :per][:, None, :], (1, 1, patch // LANES))
    return (block * factor).reshape(lines, patch).astype(BF16)


def word_kernel(group, total, patches, meta, coef, source_a, source_b, low_out, high_out, out_b):
    half, tokens, width = low_out.shape
    per = 2 * half
    for n, source in enumerate((source_a, source_b)):
        offset = 2 * group + n
        shape = (per, tokens, width)

        def put(value):
            if n:
                out_b[...] = value.astype(out_b.dtype)
            else:
                low_out[...] = value[:half]
                high_out[...] = value[half:]

        def run():
            if patches is None:
                value = jnp.zeros(shape, F32)
                for i in range(per):
                    factor = jnp.tile(coef[offset, i, :per][:, None, :], (1, 1, width // LANES))
                    value = value + source[i].reshape(shape) * factor
                put(value)
                return
            wide = jnp.concatenate(
                [scaled(source, coef.at[offset], i, per) for i in range(per)], axis=1
            )
            rows = patches[...].reshape(-1, width)
            put(lax.dot_general(wide, rows, NN, preferred_element_type=F32).reshape(shape))

        if offset:
            live = block_is_live(meta, total, offset)
            pl.when(live)(run)
            pl.when(jnp.logical_not(live))(lambda: put(jnp.zeros(shape, F32)))
        else:
            run()


def word_products(group, total, meta, coef, *refs):
    word_kernel(group, total, None, meta, coef, *refs)


def word_blends(group, total, patches, meta, coef, *refs):
    word_kernel(group, total, patches, meta, coef, *refs)


def word_call(group, total, shape, meta, coef, source_a, source_b, patches=()):
    part = (shape[0] // 2, *shape[1:])
    return pl.pallas_call(
        functools.partial(word_blends if patches else word_products, group, total),
        out_shape=(pltpu.VMEM(part, F32), pltpu.VMEM(part, F32), pltpu.VMEM(shape, BF16)),
        in_specs=[spec()] * (4 + len(patches)),
        out_specs=(spec(),) * 3,
        compiler_params=params(12),
        cost_estimate=tiny(),
        name=f"word_{group}",
    )(*near(*patches, meta, coef, source_a, source_b))


def patch_kernel(total, start, split, coef, *refs):
    out, result, sems = refs[-3:]
    weights, words = refs[:total], refs[total : total + sum(split)]
    count, patch, width = result.shape
    per = out.shape[0]

    def save(i):
        return pltpu.make_async_copy(result.at[i], out.at[start + i], sems.at[i])

    word_rows = jnp.concatenate(
        [w[...].reshape(w.shape[0] * w.shape[1], width) for w in words], axis=0
    )
    for i in range(count):
        tall = jnp.concatenate(
            [scaled(weights[k], coef.at[k], start + i, per) for k in range(total)], axis=0
        )
        result[i] = lax.dot_general(tall, word_rows, TN, preferred_element_type=F32).astype(BF16)
        save(i).start()
    for i in range(count):
        save(i).wait()


def patch_call(coef, weights, words, shape, start, count, prior=()):
    total = len(weights)
    flat = [piece for pieces in words for piece in pieces]
    args = (*near(coef, *weights, *flat), *prior)
    return pl.pallas_call(
        functools.partial(patch_kernel, total, start, tuple(len(p) for p in words)),
        out_shape=jax.ShapeDtypeStruct(shape, BF16),
        in_specs=[spec()] * (1 + total + len(flat)) + [spec(pl.ANY)] * len(prior),
        out_specs=spec(pl.ANY),
        scratch_shapes=[
            pltpu.VMEM((count, *shape[1:]), BF16),
            pltpu.SemaphoreType.DMA((count,)),
        ],
        input_output_aliases={len(args) - 1: 0} if prior else {},
        compiler_params=params(16),
        cost_estimate=tiny(),
        name=f"patch_{start}",
    )(*args)


def half_kernel(start, x, out):
    out[...] = x[start : start + out.shape[0]]


def half_call(start, x):
    count = x.shape[0] // 2
    return pl.pallas_call(
        functools.partial(half_kernel, start),
        out_shape=pltpu.VMEM((count, *x.shape[1:]), x.dtype),
        in_specs=[spec()],
        out_specs=spec(),
        compiler_params=params(4),
        cost_estimate=tiny(),
        name=f"half_{start}",
    )(*near(x))


def join_kernel(low, high, sibling, low_out, high_out):
    half = low.shape[0]
    low_out[...] = (low[...] + sibling[:half].astype(F32)).astype(low_out.dtype)
    high_out[...] = (high[...] + sibling[half:].astype(F32)).astype(high_out.dtype)


def join_call(name, low, high, sibling, low_type, high_type):
    return pl.pallas_call(
        join_kernel,
        out_shape=(pltpu.VMEM(low.shape, low_type), pltpu.VMEM(high.shape, high_type)),
        in_specs=[spec()] * 3,
        out_specs=(spec(),) * 2,
        compiler_params=params(4),
        cost_estimate=tiny(),
        name=name,
    )(*near(low, high, sibling))


def add_kernel(*refs):
    total = refs[0][...].astype(F32)
    for ref in refs[1:-1]:
        total = total + ref[...].astype(F32)
    refs[-1][...] = total.astype(refs[-1].dtype)


def add_call(name, dtype, *arrays):
    return pl.pallas_call(
        add_kernel,
        out_shape=pltpu.VMEM(arrays[0].shape, dtype),
        in_specs=[spec()] * len(arrays),
        out_specs=spec(),
        compiler_params=params(4),
        cost_estimate=tiny(),
        name=name,
    )(*near(*arrays))


def total_kernel(lows, highs, *refs):
    out = refs[-1]
    half = out.shape[0] // 2
    wholes = refs[lows + highs : -1]
    for n, part in enumerate((refs[:lows], refs[lows : lows + highs])):
        here = slice(half * n, half * (n + 1))
        total = part[0][...].astype(F32)
        for ref in part[1:]:
            total = total + ref[...].astype(F32)
        for ref in wholes:
            total = total + ref[here].astype(F32)
        out[here] = total.astype(out.dtype)


def total_call(name, lows, highs, wholes, out):
    return pl.pallas_call(
        functools.partial(total_kernel, len(lows), len(highs)),
        out_shape=out,
        in_specs=[spec()] * (len(lows) + len(highs) + len(wholes)),
        out_specs=spec(),
        compiler_params=params(8),
        cost_estimate=tiny(),
        name=name,
    )(*near(*lows, *highs, *wholes))


def finish_kernel(lows, highs, mine, other, *refs):
    word_out, loss_out, temp_out = refs[-3:]
    total_kernel(lows, highs, *refs[:-2])
    total = mine[...] + other[...]
    loss_out[0] = total[0, 0]
    temp_out[0] = total[1, 0]


def finish_call(mine, other, lows, highs, wholes, shape):
    one = jax.ShapeDtypeStruct((1,), F32)
    return pl.pallas_call(
        functools.partial(finish_kernel, len(lows), len(highs)),
        out_shape=(jax.ShapeDtypeStruct(shape, BF16), one, one),
        in_specs=[spec()] * (2 + len(lows) + len(highs) + len(wholes)),
        out_specs=(spec(), spec(pltpu.SMEM), spec(pltpu.SMEM)),
        compiler_params=params(8),
        cost_estimate=tiny(),
        name="finish",
    )(*near(mine, other, *lows, *highs, *wholes))


def body(patches, words, natural_sharpness_exponent, candidates, counts):
    total = lax.axis_size("cap")
    rows = lax.axis_size("img")
    per, patch, width = patches.shape
    images = per * total * rows
    groups = total // 2
    half = per // 2
    bits = [1 << n for n in range(groups.bit_length() - 1)]
    barrier = lax.optimization_barrier

    def low_bit(g):
        return g & -g

    def high_bit(g):
        return 1 << (g.bit_length() - 1)

    def hop(x, offset):
        return lax.ppermute(x, "cap", [(i, i ^ offset) for i in range(total)])

    words_at = [None] * total
    words_at[0] = (words,)
    for b in bits:
        words_at[2 * b] = (hop(words, 2 * b),)
    words_at[1] = (hop(words, 1),)

    meta = turned = None
    weights, scores, products = [], [], {}

    def forward(k):
        nonlocal meta, patches, turned
        if k:
            extra = (meta, scores[-1])
        else:
            extra = (jnp.transpose(candidates, (2, 0, 1)), counts, natural_sharpness_exponent)
        product = k < 2 or k // 2 in bits
        made = forward_call(k, total, product, patches, turned, words_at[k], extra)
        if not k:
            meta, patches, turned, near_words = made[-4:]
            words_at[0] = (near_words,)
        weights.append(made[0])
        scores.append(made[1])
        if product:
            products[k] = made[2]

    forward(0)
    forward(1)
    for b in bits:
        words_at[2 * b] = barrier((words_at[2 * b][0], scores[-1]))[:1]

    def part(g, side):
        pieces = words_at[2 * g]
        return pieces[side] if len(pieces) == 2 else half_call(side * half, pieces[0])

    for g in range(1, groups):
        if words_at[2 * g] is None:
            words_at[2 * g] = (
                hop(part(g ^ high_bit(g), 0), 2 * high_bit(g)),
                hop(part(g ^ low_bit(g), 1), 2 * low_bit(g)),
            )
    for b in bits:
        words_at[2 * b + 1] = (hop(words_at[2 * b][0], 1),)
    sequence = bits + [g for g in range(1, groups) if g not in bits]
    order = [0, 1] + [2 * g + n for g in sequence for n in (0, 1)]
    done = 2
    for g in sequence:
        if words_at[2 * g + 1] is None:
            *pieces, _ = barrier((*words_at[2 * g], scores[-1]))
            words_at[2 * g] = tuple(pieces)
            words_at[2 * g + 1] = tuple(hop(x, 1) for x in pieces)
        forward(2 * g)
        forward(2 * g + 1)
    by_offset = dict(zip(order, weights))
    weights = [by_offset[k] for k in range(total)]
    scores = scores[-1]

    pair = pair_call(per, scores, hop(scores, 1))
    tiles = [pair] + [hop(pair, 2 * g) for g in range(1, groups)]
    coef, sums = stats_call(images, per, width, meta, tiles)

    lows = [[] for _ in range(groups)]
    highs = [[] for _ in range(groups)]
    wholes = [[] for _ in range(groups)]
    mixed = []

    def word(g, coef):
        if 2 * g in products:
            sources = (products[2 * g], products[2 * g + 1])
        else:
            sources = (weights[2 * g], weights[2 * g + 1], (patches,))
        low, high, theirs = word_call(g, total, words.shape, meta, coef, *sources)
        lows[g].append(low)
        highs[g].append(high)
        wholes[g].append(hop(theirs, 1))

    far = [g for g in range(1, groups) if g not in bits]
    for g in sorted(far, key=lambda g: -bin(g).count("1")) + bits:
        word(g, coef)
    for g in far + bits:
        low, high = join_call(
            f"join_{g}",
            lows[g].pop(),
            highs[g].pop(),
            wholes[g].pop(),
            BF16 if g & 1 else F32,
            BF16 if g & bits[-1] else F32,
        )
        lows[g].append(low)
        highs[g].append(high)
    word(0, barrier((coef, *(lows[b][0] for b in bits), *(highs[b][0] for b in bits)))[0])

    step = 1
    while 2 * step < rows:
        other = lax.ppermute(sums, "img", [(i, i ^ step) for i in range(rows)])
        sums = add_call(f"sums_{step}", F32, sums, other)
        step *= 2

    early = []

    def pass_on(store, g, b, name):
        terms = store[g]
        value = terms[0]
        if len(terms) > 1:
            *terms, _ = barrier((*terms, sums))
            value = add_call(name, BF16, *terms)
            mixed.append(value)
        moved = hop(value, 2 * b)
        if len(terms) == 1 and g == b:
            early.append(moved)
        store[g ^ b].append(moved)

    for b in bits:
        for g in range(groups - 1, 0, -1):
            if low_bit(g) == b:
                pass_on(lows, g, b, f"low_{g}")
    for b in reversed(bits):
        for g in range(groups - 1, 0, -1):
            if high_bit(g) == b:
                pass_on(highs, g, b, f"high_{g}")

    late_coef, *_ = barrier((coef, *mixed))
    patch_grad = patch_call(late_coef, weights, words_at, patches.shape, 0, per // 2)
    sums, patch_grad = barrier((sums, patch_grad))
    other = lax.ppermute(sums, "img", [(i, i ^ step) for i in range(rows)])
    late_coef, *_ = barrier((late_coef, *early))
    patch_grad = patch_call(
        late_coef, weights, words_at, patches.shape, per // 2, per - per // 2, (patch_grad,)
    )
    word_grad, loss, temp = finish_call(
        sums, other, lows[0], highs[0], wholes[0], words.shape
    )
    return patch_grad, word_grad, loss, temp


def solution(mesh):
    placed = (P(("img", "cap"), None, None), P(("img", "cap"), None, None), P(), P(), P())
    return jax.shard_map(
        body,
        mesh=mesh,
        in_specs=placed,
        out_specs=(P(("img", "cap"), None, None), P(("img", "cap"), None, None), P(), P()),
        check_vma=False,
    )
```

```python
import functools
import math

import jax
import jax.numpy as jnp
from jax import lax
from jax.experimental import pallas as pl
from jax.experimental.pallas import tpu as pltpu
from jax.sharding import PartitionSpec as P

sharpness = 4.0
loss_scale = 65536.0
far_below = -1e30
F32 = jnp.float32
BF16 = jnp.bfloat16
LANES = 128
ROWS = 8

NN = (((1,), (0,)), ((), ()))
TN = (((0,), (0,)), ((), ()))


def spec(space=pltpu.VMEM):
    return pl.BlockSpec(memory_space=space)


def near(*arrays):
    return tuple(pltpu.with_memory_space_constraint(x, pltpu.VMEM) for x in arrays)


def tiny():
    return pl.CostEstimate(flops=1, bytes_accessed=1, transcendentals=0)


def params(mib):
    return pltpu.CompilerParams(vmem_limit_bytes=mib << 20)


def fill_meta(cands, counts, nse, per, total, meta):
    row = lax.axis_index("img")
    me = lax.axis_index("cap")
    slots = cands.shape[0]
    sub = lax.broadcasted_iota(jnp.int32, (ROWS, LANES), 0)
    lane = lax.broadcasted_iota(jnp.int32, (ROWS, LANES), 1)
    column = lane // per
    first = sub < per
    for g in range(total // 2):
        even, odd = me ^ (2 * g), me ^ (2 * g + 1)
        live = jnp.zeros((ROWS, LANES), F32)
        for s in range(slots):
            here = jnp.where(s < counts[row, even], cands[s, row, even], -1)
            there = jnp.where(s < counts[row, odd], cands[s, row, odd], -1)
            live = jnp.where(column == jnp.where(first, here, there), 1.0, live)
        meta[g] = jnp.where(sub < 2 * per, live, 0.0)
    for part in range(total // ROWS):
        live = jnp.zeros((ROWS, LANES), F32)
        for s in range(slots):
            target = jnp.where(s < counts[row, me], cands[s, row, me], -1)
            live = jnp.where((me ^ (sub + ROWS * part)) == target, 1.0, live)
        meta[total // 2 + part] = live
    meta[meta.shape[0] - 1] = jnp.exp(jnp.full((ROWS, LANES), nse[0], F32))


def block_is_live(meta, total, offset):
    return meta[total // 2 + offset // ROWS, offset % ROWS, 0] > 0.0


def forward_kernel(offset, pieces, total, product, *refs):
    fetched = ()
    if offset:
        meta, patches, turned, prior, *words = refs[: 4 + pieces]
        outs = refs[4 + pieces :]
    else:
        cands_far, counts_far, nse, patches_far, words_far = refs[:5]
        *outs, patches, turned, near_words, cands, counts, sems = refs[5:]
        words = [near_words]
        moves = [(cands_far, cands), (counts_far, counts), (words_far, near_words)]
        moves += [(patches_far.at[i], patches.at[i]) for i in range(patches.shape[0])]
        copies = [pltpu.make_async_copy(a, b, sems.at[n]) for n, (a, b) in enumerate(moves)]
        for copy in copies[2:]:
            copy.start()
        for copy in copies[:2]:
            copy.start()
        fetched = copies[3:]
    weights_out, scores_out = outs[:2]
    me = lax.axis_index("cap")
    column = me ^ offset
    per, patch, width = patches.shape
    tokens = words[0].shape[1]
    lines = per * tokens
    scale = sharpness * width**-0.5 * math.log2(math.e)

    def start():
        scores_out[...] = prior[...] if offset else jnp.zeros(scores_out.shape, F32)

    start()
    if not offset:
        copies[2].wait()

    def score():
        sub = lax.broadcasted_iota(jnp.int32, (ROWS, LANES), 0)
        lane = lax.broadcasted_iota(jnp.int32, (ROWS, LANES), 1)
        spot = lane == column * per + sub

        def place(i, over_words, over_patches):
            part = jnp.sum(over_words, axis=1, keepdims=True) * (1.0 / patch)
            part = part + over_patches * (1.0 / tokens)
            part = part * (0.5 * math.log(2.0) / sharpness)
            part = jnp.concatenate([part, jnp.zeros((ROWS - per, 1), F32)], axis=0)
            line = jnp.sum(jnp.where(spot & (sub < per), part, 0.0), axis=0, keepdims=True)
            return jnp.where(sub == i, line, 0.0)

        word_rows = jnp.concatenate(
            [w[...].reshape(w.shape[0] * tokens, width) for w in words], axis=0
        )
        low = high = None
        tile = jnp.zeros((ROWS, LANES), F32)
        for i in range(per):
            if fetched:
                fetched[i].wait()
                turned[i] = patches[i].T
            raw = lax.dot_general(word_rows, turned[i], NN, preferred_element_type=F32)
            mass = jnp.exp2(raw * scale)
            mass3 = mass.reshape(per, tokens, patch)
            word_sum = jnp.sum(mass3, axis=1)
            patch_sum = jnp.sum(mass, axis=1, keepdims=True)
            least = jnp.minimum(
                jnp.min(word_sum, axis=0, keepdims=True),
                jnp.min(patch_sum, axis=0, keepdims=True),
            )
            most = jnp.maximum(
                jnp.max(word_sum, axis=0, keepdims=True),
                jnp.max(patch_sum, axis=0, keepdims=True),
            )
            low = least if low is None else jnp.minimum(low, least)
            high = most if high is None else jnp.maximum(high, most)
            word_part = (0.5 / patch) / word_sum
            patch_part = (0.5 / tokens) / patch_sum
            blended = mass3 * (word_part[:, None, :] + patch_part.reshape(per, tokens, 1))
            weights_out[i] = blended.reshape(lines, patch).astype(BF16)
            patch_logs = jnp.sum(jnp.log2(patch_sum).reshape(per, tokens, 1), axis=1)
            tile = tile + place(i, jnp.log2(word_sum), patch_logs)
        scores_out[...] += tile
        safe = (jnp.min(low) > 2.0**-90) & (jnp.max(high) < 2.0**120)

        @pl.when(jnp.logical_not(safe))
        def _():
            start()

            def image(i, carry):
                raw = lax.dot_general(word_rows, turned[i], NN, preferred_element_type=F32)
                lifted = raw * scale
                lifted3 = lifted.reshape(per, tokens, patch)
                word_top = jnp.max(lifted3, axis=1)
                patch_top = jnp.max(lifted, axis=1, keepdims=True)
                word_mass = jnp.exp2(lifted3 - word_top[:, None, :])
                patch_mass = jnp.exp2(lifted - patch_top).reshape(per, tokens, patch)
                word_sum = jnp.sum(word_mass, axis=1)
                patch_sum = jnp.sum(patch_mass, axis=2, keepdims=True)
                word_part = (0.5 / patch) / word_sum
                patch_part = (0.5 / tokens) / patch_sum
                blended = word_mass * word_part[:, None, :] + patch_mass * patch_part
                weights_out[i] = blended.reshape(lines, patch).astype(BF16)
                patch_logs = jnp.sum(
                    patch_top.reshape(per, tokens, 1) + jnp.log2(patch_sum), axis=1
                )
                scores_out[...] += place(i, word_top + jnp.log2(word_sum), patch_logs)
                return carry

            lax.fori_loop(0, per, image, 0)

        if product:
            for i in range(per):
                outs[2][i] = lax.dot_general(
                    weights_out[i], patches[i], NN, preferred_element_type=F32
                )

    if offset:
        live = block_is_live(meta, total, offset)
        pl.when(live)(score)

        @pl.when(jnp.logical_not(live))
        def _():
            weights_out[...] = jnp.zeros(weights_out.shape, weights_out.dtype)

    else:
        score()
        for copy in copies[:2]:
            copy.wait()
        fill_meta(cands, counts, nse, per, total, outs[-1])


def forward_call(offset, total, product, patches, turned, words, extra):
    per, patch, width = patches.shape
    lines = per * words[0].shape[1]
    shapes = (pltpu.VMEM((per, lines, patch), BF16), pltpu.VMEM((ROWS, LANES), F32))
    scratch = []
    if product:
        shapes += (pltpu.VMEM((per, lines, width), F32),)
    if offset:
        meta, prior = extra
        args = near(meta, patches, turned, prior, *words)
        specs = [spec()] * len(args)
    else:
        cands, counts, nse = extra
        args = [cands, counts, patches, *words]
        args = [pltpu.with_memory_space_constraint(x, pltpu.HBM) for x in args]
        args.insert(2, nse)
        specs = [spec(pl.ANY)] * 2 + [spec(pltpu.SMEM)] + [spec(pl.ANY)] * 2
        shapes += (
            pltpu.VMEM((total // 2 + total // ROWS + 1, ROWS, LANES), F32),
            pltpu.VMEM(patches.shape, BF16),
            pltpu.VMEM((per, width, patch), BF16),
            pltpu.VMEM(words[0].shape, BF16),
        )
        scratch = [
            pltpu.SMEM(cands.shape, jnp.int32),
            pltpu.SMEM(counts.shape, jnp.int32),
            pltpu.SemaphoreType.DMA((3 + per,)),
        ]
    return pl.pallas_call(
        functools.partial(forward_kernel, offset, len(words), total, product),
        out_shape=shapes,
        in_specs=specs,
        out_specs=(spec(),) * len(shapes),
        scratch_shapes=scratch,
        compiler_params=params(12),
        cost_estimate=tiny(),
        name=f"forward_{offset}",
    )(*args)


def stats_kernel(total, images, per, width, meta, *refs):
    tiles = refs[: total // 2]
    coef_out, sums_out = refs[total // 2 :]
    me = lax.axis_index("cap")
    sub = lax.broadcasted_iota(jnp.int32, (ROWS, LANES), 0)
    lane = lax.broadcasted_iota(jnp.int32, (ROWS, LANES), 1)
    first = sub < per
    image = jnp.where(first, sub, sub - per)
    softness = meta[meta.shape[0] - 1]
    kept, lives, marks = [], [], []
    peak = jnp.full((1, LANES), far_below, F32)
    for g in range(total // 2):
        even, odd = me ^ (2 * g), me ^ (2 * g + 1)
        live = meta[g] > 0.0
        masked = jnp.where(live, tiles[g][...] * softness, far_below)
        kept.append(masked)
        lives.append(live)
        marks.append(live & (lane == jnp.where(first, even, odd) * per + image))
        peak = jnp.maximum(peak, jnp.max(masked, axis=0, keepdims=True))
    mass = jnp.zeros((1, LANES), F32)
    for masked, live in zip(kept, lives):
        mass = mass + jnp.sum(
            jnp.where(live, jnp.exp(masked - peak), 0.0), axis=0, keepdims=True
        )
    col_ok = lane[:1] < total * per
    col_lse = jnp.where(col_ok, peak + jnp.log(jnp.where(col_ok, mass, 1.0)), 0.0)
    loss = jnp.where(sub == 0, col_lse, 0.0)
    temp = jnp.zeros((ROWS, LANES), F32)
    pulls = []
    for masked, live, mark in zip(kept, lives, marks):
        top = jnp.max(masked, axis=1, keepdims=True)
        part = jnp.sum(jnp.where(live, jnp.exp(masked - top), 0.0), axis=1, keepdims=True)
        row_lse = top + jnp.log(jnp.where(sub[:, :1] < 2 * per, part, 1.0))
        pull = jnp.where(
            live,
            (0.5 / images)
            * (jnp.exp(masked - row_lse) + jnp.exp(masked - col_lse) - jnp.where(mark, 2.0, 0.0)),
            0.0,
        )
        pulls.append(pull)
        temp = temp + jnp.where(live, pull * masked, 0.0)
        loss = loss + jnp.where((lane == 0) & (sub < 2 * per), row_lse, 0.0)
        loss = loss - jnp.where(mark, 2.0 * masked, 0.0)
    loss_total = jnp.sum(loss) * (0.5 / images)
    temp_total = jnp.sum(temp)
    sums_out[...] = jnp.where(sub == 0, loss_total, temp_total)
    factor = pulls[0] * softness * (loss_scale * width**-0.5)
    for k in range(total):
        spot = (lane == (me ^ k) * per + sub) & first
        for i in range(per):
            line = jnp.broadcast_to(factor[i : i + 1], (ROWS, LANES))
            value = jnp.sum(jnp.where(spot, line, 0.0), axis=1, keepdims=True)
            coef_out[k, i] = jnp.broadcast_to(value, (ROWS, LANES))


def stats_call(images, per, width, meta, tiles):
    total = 2 * len(tiles)
    return pl.pallas_call(
        functools.partial(stats_kernel, total, images, per, width),
        out_shape=(
            pltpu.VMEM((total, per, ROWS, LANES), F32),
            pltpu.VMEM((ROWS, LANES), F32),
        ),
        in_specs=[spec()] * (1 + len(tiles)),
        out_specs=(spec(), spec()),
        compiler_params=params(4),
        cost_estimate=tiny(),
        name="stats",
    )(*near(meta, *tiles))


def pair_kernel(per, own, other, out):
    sub = lax.broadcasted_iota(jnp.int32, (ROWS, LANES), 0)
    moved = jnp.concatenate([other[...]] * 2, axis=0)[ROWS - per : 2 * ROWS - per]
    out[...] = jnp.where(sub < per, own[...], moved)


def pair_call(per, own, other):
    return pl.pallas_call(
        functools.partial(pair_kernel, per),
        out_shape=pltpu.VMEM((ROWS, LANES), F32),
        in_specs=[spec()] * 2,
        out_specs=spec(),
        compiler_params=params(4),
        cost_estimate=tiny(),
        name="pair",
    )(*near(own, other))


def scaled(weights, coef, i, per):
    lines, patch = weights.shape[1:]
    block = weights[i].astype(F32).reshape(per, lines // per, patch)
    factor = jnp.tile(coef[i, :per][:, None, :], (1, 1, patch // LANES))
    return (block * factor).reshape(lines, patch).astype(BF16)


def word_kernel(group, total, patches, meta, coef, source_a, source_b, low_out, high_out, out_b):
    half, tokens, width = low_out.shape
    per = 2 * half
    for n, source in enumerate((source_a, source_b)):
        offset = 2 * group + n
        shape = (per, tokens, width)

        def put(value):
            if n:
                out_b[...] = value.astype(out_b.dtype)
            else:
                low_out[...] = value[:half]
                high_out[...] = value[half:]

        def run():
            if patches is None:
                value = jnp.zeros(shape, F32)
                for i in range(per):
                    factor = jnp.tile(coef[offset, i, :per][:, None, :], (1, 1, width // LANES))
                    value = value + source[i].reshape(shape) * factor
                put(value)
                return
            wide = jnp.concatenate(
                [scaled(source, coef.at[offset], i, per) for i in range(per)], axis=1
            )
            rows = patches[...].reshape(-1, width)
            put(lax.dot_general(wide, rows, NN, preferred_element_type=F32).reshape(shape))

        if offset:
            live = block_is_live(meta, total, offset)
            pl.when(live)(run)
            pl.when(jnp.logical_not(live))(lambda: put(jnp.zeros(shape, F32)))
        else:
            run()


def word_products(group, total, meta, coef, *refs):
    word_kernel(group, total, None, meta, coef, *refs)


def word_blends(group, total, patches, meta, coef, *refs):
    word_kernel(group, total, patches, meta, coef, *refs)


def word_call(group, total, shape, meta, coef, source_a, source_b, patches=()):
    part = (shape[0] // 2, *shape[1:])
    return pl.pallas_call(
        functools.partial(word_blends if patches else word_products, group, total),
        out_shape=(pltpu.VMEM(part, F32), pltpu.VMEM(part, F32), pltpu.VMEM(shape, BF16)),
        in_specs=[spec()] * (4 + len(patches)),
        out_specs=(spec(),) * 3,
        compiler_params=params(12),
        cost_estimate=tiny(),
        name=f"word_{group}",
    )(*near(*patches, meta, coef, source_a, source_b))


def patch_kernel(total, start, split, coef, *refs):
    out, result, sems = refs[-3:]
    weights, words = refs[:total], refs[total : total + sum(split)]
    count, patch, width = result.shape
    per = out.shape[0]

    def save(i):
        return pltpu.make_async_copy(result.at[i], out.at[start + i], sems.at[i])

    word_rows = jnp.concatenate(
        [w[...].reshape(w.shape[0] * w.shape[1], width) for w in words], axis=0
    )
    for i in range(count):
        tall = jnp.concatenate(
            [scaled(weights[k], coef.at[k], start + i, per) for k in range(total)], axis=0
        )
        result[i] = lax.dot_general(tall, word_rows, TN, preferred_element_type=F32).astype(BF16)
        save(i).start()
    for i in range(count):
        save(i).wait()


def patch_call(coef, weights, words, shape, start, count, prior=()):
    total = len(weights)
    flat = [piece for pieces in words for piece in pieces]
    args = (*near(coef, *weights, *flat), *prior)
    return pl.pallas_call(
        functools.partial(patch_kernel, total, start, tuple(len(p) for p in words)),
        out_shape=jax.ShapeDtypeStruct(shape, BF16),
        in_specs=[spec()] * (1 + total + len(flat)) + [spec(pl.ANY)] * len(prior),
        out_specs=spec(pl.ANY),
        scratch_shapes=[
            pltpu.VMEM((count, *shape[1:]), BF16),
            pltpu.SemaphoreType.DMA((count,)),
        ],
        input_output_aliases={len(args) - 1: 0} if prior else {},
        compiler_params=params(16),
        cost_estimate=tiny(),
        name=f"patch_{start}",
    )(*args)


def half_kernel(start, x, out):
    out[...] = x[start : start + out.shape[0]]


def half_call(start, x):
    count = x.shape[0] // 2
    return pl.pallas_call(
        functools.partial(half_kernel, start),
        out_shape=pltpu.VMEM((count, *x.shape[1:]), x.dtype),
        in_specs=[spec()],
        out_specs=spec(),
        compiler_params=params(4),
        cost_estimate=tiny(),
        name=f"half_{start}",
    )(*near(x))


def join_kernel(low, high, sibling, low_out, high_out):
    half = low.shape[0]
    low_out[...] = (low[...] + sibling[:half].astype(F32)).astype(low_out.dtype)
    high_out[...] = (high[...] + sibling[half:].astype(F32)).astype(high_out.dtype)


def join_call(name, low, high, sibling, low_type, high_type):
    return pl.pallas_call(
        join_kernel,
        out_shape=(pltpu.VMEM(low.shape, low_type), pltpu.VMEM(high.shape, high_type)),
        in_specs=[spec()] * 3,
        out_specs=(spec(),) * 2,
        compiler_params=params(4),
        cost_estimate=tiny(),
        name=name,
    )(*near(low, high, sibling))


def add_kernel(*refs):
    total = refs[0][...].astype(F32)
    for ref in refs[1:-1]:
        total = total + ref[...].astype(F32)
    refs[-1][...] = total.astype(refs[-1].dtype)


def add_call(name, dtype, *arrays):
    return pl.pallas_call(
        add_kernel,
        out_shape=pltpu.VMEM(arrays[0].shape, dtype),
        in_specs=[spec()] * len(arrays),
        out_specs=spec(),
        compiler_params=params(4),
        cost_estimate=tiny(),
        name=name,
    )(*near(*arrays))


def total_kernel(lows, highs, *refs):
    out = refs[-1]
    half = out.shape[0] // 2
    wholes = refs[lows + highs : -1]
    for n, part in enumerate((refs[:lows], refs[lows : lows + highs])):
        here = slice(half * n, half * (n + 1))
        total = part[0][...].astype(F32)
        for ref in part[1:]:
            total = total + ref[...].astype(F32)
        for ref in wholes:
            total = total + ref[here].astype(F32)
        out[here] = total.astype(out.dtype)


def total_call(name, lows, highs, wholes, out):
    return pl.pallas_call(
        functools.partial(total_kernel, len(lows), len(highs)),
        out_shape=out,
        in_specs=[spec()] * (len(lows) + len(highs) + len(wholes)),
        out_specs=spec(),
        compiler_params=params(8),
        cost_estimate=tiny(),
        name=name,
    )(*near(*lows, *highs, *wholes))


def finish_kernel(lows, highs, mine, other, *refs):
    word_out, loss_out, temp_out = refs[-3:]
    total_kernel(lows, highs, *refs[:-2])
    total = mine[...] + other[...]
    loss_out[0] = total[0, 0]
    temp_out[0] = total[1, 0]


def finish_call(mine, other, lows, highs, wholes, shape):
    one = jax.ShapeDtypeStruct((1,), F32)
    return pl.pallas_call(
        functools.partial(finish_kernel, len(lows), len(highs)),
        out_shape=(jax.ShapeDtypeStruct(shape, BF16), one, one),
        in_specs=[spec()] * (2 + len(lows) + len(highs) + len(wholes)),
        out_specs=(spec(), spec(pltpu.SMEM), spec(pltpu.SMEM)),
        compiler_params=params(8),
        cost_estimate=tiny(),
        name="finish",
    )(*near(mine, other, *lows, *highs, *wholes))


def body(patches, words, natural_sharpness_exponent, candidates, counts):
    total = lax.axis_size("cap")
    rows = lax.axis_size("img")
    per, patch, width = patches.shape
    images = per * total * rows
    groups = total // 2
    half = per // 2
    bits = [1 << n for n in range(groups.bit_length() - 1)]
    barrier = lax.optimization_barrier

    def low_bit(g):
        return g & -g

    def high_bit(g):
        return 1 << (g.bit_length() - 1)

    def hop(x, offset):
        return lax.ppermute(x, "cap", [(i, i ^ offset) for i in range(total)])

    words_at = [None] * total
    words_at[0] = (words,)
    for b in bits:
        words_at[2 * b] = (hop(words, 2 * b),)
    words_at[1] = (hop(words, 1),)

    meta = turned = None
    weights, scores, products = [], [], {}

    def forward(k):
        nonlocal meta, patches, turned
        if k:
            extra = (meta, scores[-1])
        else:
            extra = (jnp.transpose(candidates, (2, 0, 1)), counts, natural_sharpness_exponent)
        product = k < 2 or k // 2 in bits
        made = forward_call(k, total, product, patches, turned, words_at[k], extra)
        if not k:
            meta, patches, turned, near_words = made[-4:]
            words_at[0] = (near_words,)
        weights.append(made[0])
        scores.append(made[1])
        if product:
            products[k] = made[2]

    forward(0)
    forward(1)
    for b in bits:
        words_at[2 * b] = barrier((words_at[2 * b][0], scores[-1]))[:1]

    def part(g, side):
        pieces = words_at[2 * g]
        return pieces[side] if len(pieces) == 2 else half_call(side * half, pieces[0])

    for g in range(1, groups):
        if words_at[2 * g] is None:
            words_at[2 * g] = (
                hop(part(g ^ high_bit(g), 0), 2 * high_bit(g)),
                hop(part(g ^ low_bit(g), 1), 2 * low_bit(g)),
            )
    for b in bits:
        words_at[2 * b + 1] = (hop(words_at[2 * b][0], 1),)
    sequence = bits + [g for g in range(1, groups) if g not in bits]
    order = [0, 1] + [2 * g + n for g in sequence for n in (0, 1)]
    done = 2
    for g in sequence:
        if words_at[2 * g + 1] is None:
            *pieces, _ = barrier((*words_at[2 * g], scores[-1]))
            words_at[2 * g] = tuple(pieces)
            words_at[2 * g + 1] = tuple(hop(x, 1) for x in pieces)
        forward(2 * g)
        forward(2 * g + 1)
    by_offset = dict(zip(order, weights))
    weights = [by_offset[k] for k in range(total)]
    scores = scores[-1]

    pair = pair_call(per, scores, hop(scores, 1))
    tiles = [pair] + [hop(pair, 2 * g) for g in range(1, groups)]
    coef, sums = stats_call(images, per, width, meta, tiles)

    lows = [[] for _ in range(groups)]
    highs = [[] for _ in range(groups)]
    wholes = [[] for _ in range(groups)]
    mixed = []

    def word(g, coef):
        if 2 * g in products:
            sources = (products[2 * g], products[2 * g + 1])
        else:
            sources = (weights[2 * g], weights[2 * g + 1], (patches,))
        low, high, theirs = word_call(g, total, words.shape, meta, coef, *sources)
        lows[g].append(low)
        highs[g].append(high)
        wholes[g].append(hop(theirs, 1))

    far = [g for g in range(1, groups) if g not in bits]
    for g in sorted(far, key=lambda g: -bin(g).count("1")) + bits:
        word(g, coef)
    for g in far + bits:
        low, high = join_call(
            f"join_{g}",
            lows[g].pop(),
            highs[g].pop(),
            wholes[g].pop(),
            BF16 if g & 1 else F32,
            BF16 if g & bits[-1] else F32,
        )
        lows[g].append(low)
        highs[g].append(high)
    word(0, barrier((coef, *(lows[b][0] for b in bits), *(highs[b][0] for b in bits)))[0])

    step = 1
    while 2 * step < rows:
        other = lax.ppermute(sums, "img", [(i, i ^ step) for i in range(rows)])
        sums = add_call(f"sums_{step}", F32, sums, other)
        step *= 2

    early = []

    def pass_on(store, g, b, name):
        terms = store[g]
        value = terms[0]
        if len(terms) > 1:
            *terms, _ = barrier((*terms, sums))
            value = add_call(name, BF16, *terms)
            mixed.append(value)
        moved = hop(value, 2 * b)
        if len(terms) == 1 and g == b:
            early.append(moved)
        store[g ^ b].append(moved)

    for b in bits:
        for g in range(groups - 1, 0, -1):
            if low_bit(g) == b:
                pass_on(lows, g, b, f"low_{g}")
    for b in reversed(bits):
        for g in range(groups - 1, 0, -1):
            if high_bit(g) == b:
                pass_on(highs, g, b, f"high_{g}")

    late_coef, *_ = barrier((coef, *mixed))
    patch_grad = patch_call(late_coef, weights, words_at, patches.shape, 0, per // 2)
    sums, patch_grad = barrier((sums, patch_grad))
    other = lax.ppermute(sums, "img", [(i, i ^ step) for i in range(rows)])
    late_coef, *_ = barrier((late_coef, *early[:1]))
    patch_grad = patch_call(
        late_coef, weights, words_at, patches.shape, per // 2, per - per // 2, (patch_grad,)
    )
    word_grad, loss, temp = finish_call(
        sums, other, lows[0], highs[0], wholes[0], words.shape
    )
    return patch_grad, word_grad, loss, temp


def solution(mesh):
    placed = (P(("img", "cap"), None, None), P(("img", "cap"), None, None), P(), P(), P())
    return jax.shard_map(
        body,
        mesh=mesh,
        in_specs=placed,
        out_specs=(P(("img", "cap"), None, None), P(("img", "cap"), None, None), P(), P()),
        check_vma=False,
    )
```
